256 devices in a mesh: dp: 16 (over y, z_hi, core), mp: 16 (over x, z_lo).
Axes of the slice: x: 4, y: 4, z: 8 (z_hi: 2, z_lo: 4; z = z_hi * 4 + z_lo), core: 2. Of those that a mesh axis runs over, the one named last changes fastest.
Arguments:
- skip_stream_arriving: float32 [4096, 2304], P('dp', 'mp'), may hold values from -170 to 170
- chosen_specialists: int32 [4096, 2], P('dp'), may hold values from 0 to 3, all different within a row; in each aligned block of 256 rows (0 to 255, 256 to 511, ...) at most 160 rows name the same one
- sequence_piece_tallies: int32 [16, 4], P('dp'), may hold values from 1 to 128, 256 in all within a row
- premix_rmsnorm_gain: float32 [2304], P('mp'), may hold values from 0.1 to 1.9
- dispatcher_weights: bfloat16 [2304, 4], replicated, may hold values from -0.125 to 0.125
- specialist_switch_weights: bfloat16 [4, 2304, 5760], P(None, 'dp', 'mp'), may hold values from -0.125 to 0.125
- specialist_expand_weights: bfloat16 [4, 2304, 5760], P(None, 'dp', 'mp'), may hold values from -0.125 to 0.125
- specialist_contract_weights: bfloat16 [4, 5760, 2304], P(None, 'mp', 'dp'), may hold values from -0.109375 to 0.109375
- terminal_rmsnorm_gain: float32 [2304], replicated, may hold values from 0.1 to 1.9
- lexicon_projector_weights: bfloat16 [2304, 131072], P(None, ('dp', 'mp')), may hold values from -12 to 12
- softness_per_sequence: float32 [64], replicated, may hold values from 0.02 to 1.5
Outputs:
- new_hidden: float32 [4096, 2304], P('dp', 'mp')
- logprobs: float32 [64, 131072], P(None, ('dp', 'mp'))
The draws below stay inside these ranges and needn't reach their ends.
Inputs may be any that keep to these rules, and one draw needn't show every extreme that they name: `chosen_specialists`: in the 256 rows of each data group no expert is named by more than 160 rows, a bound that some block reaches. `sequence_piece_tallies`: each row sums to 256; its largest entry is 128.
All inputs are finite; a program needn't handle non-finite values.
Results may differ from the reference program's by a relative error of at most 0.0014.
Values may be sent and summed in bfloat16 or wider, within the bound.
A program may use at most 128 MiB of HBM per device.

```python
import math
import jax
import jax.numpy as jnp
import numpy as np
from jax import lax

EMBED_DIMENSION = 2304
FF = 5760
EXPERTS = 4
TOP = 2
TOK_GRP = 256
CAP = 160
REQ_GRP = 4
TOKENS = 4096
REQS = 64
VOCAB = 131072
N_DP = 16
N_MP = 16


def draw_skip_stream_arriving(key, part):
    base_key, scale_key = jax.random.split(key, 2)
    spread = jnp.exp(jax.random.uniform(scale_key, (EMBED_DIMENSION,), jnp.float32, -1.15, 1.15))
    rising = 0.5 + jnp.arange(EMBED_DIMENSION, dtype=jnp.float32) / EMBED_DIMENSION
    values = jnp.clip(jax.random.normal(base_key, (TOKENS, EMBED_DIMENSION), jnp.float32), -6.0, 6.0)
    return values * spread * rising


def draw_lexicon_projector_weights(key, part):
    base_key, scale_key = jax.random.split(key, 2)
    column_scale = jnp.exp(jax.random.uniform(scale_key, (1, VOCAB), jnp.float32, 0.0, 2.3))
    values = jnp.clip(jax.random.normal(base_key, (EMBED_DIMENSION, VOCAB), jnp.float32), -6.0, 6.0)
    return (0.2 * values * column_scale).astype(jnp.bfloat16)


def draw_softness_per_sequence(key, part):
    return jnp.exp(jax.random.uniform(key, (REQS,), jnp.float32, -0.69, 0.405))


def spiked(array, stream_key, source, target, parts, factor):
    def block_of(axis_at):
        return (jnp.arange(array.shape[axis_at]) // (array.shape[axis_at] // parts)).reshape((-1,) + (1,) * (array.ndim - 1 - axis_at))

    first = jax.random.permutation(stream_key, parts)[block_of(target)]
    other_side = (block_of(target) + parts // 2) % parts
    return jnp.where((block_of(source) == first) | (block_of(source) == other_side), factor * array, array)


def steps_of(stream_key, shape, cuts, least, top_value):
    factor_of, own = 1.0, jax.random.fold_in(stream_key, 6)
    for axis_at, parts in cuts:
        draws = jnp.exp(jax.random.uniform(jax.random.fold_in(own, axis_at), (parts,), jnp.float32, least / len(cuts), top_value / len(cuts)))
        factor_of = factor_of * jnp.repeat(draws, shape[axis_at] // parts).reshape([-1 if axis == axis_at else 1 for axis in range(len(shape))])
    return factor_of


def length_profile(amount, total, bound, skew):
    loads = [(1 << 20) // math.isqrt(standing ** skew) + 1 for standing in range(2, amount + 1)]
    surplus, holding = total - bound - (amount - 1), [1] * (amount - 1)
    while surplus > 0:
        free = [i for i in range(amount - 1) if holding[i] < bound]
        whole, left = sum([loads[i] for i in free]), surplus
        for i in free:
            extra = min(bound - holding[i], max(1, left * loads[i] // whole), surplus)
            holding[i] = holding[i] + extra
            surplus = surplus - extra
    return np.array([bound] + holding)


def ragged(stream_key, number_of, total, most, lean):
    if number_of == 2:
        one = jax.random.randint(stream_key, (), max(1, total - most), min(most, total - 1) + 1)
        return jnp.stack([one, total - one])
    sizes = jnp.asarray(length_profile(number_of, total, most, lean), jnp.int32)
    twos = (number_of - 1) // 2
    donor, sink = sizes[1:1 + 2 * twos:2], sizes[2:2 + 2 * twos:2]
    room = jnp.minimum(donor - 1, most - sink)
    passed = jax.random.randint(jax.random.fold_in(stream_key, 1), (twos,), 0, 1 << 20) % (room + 1)
    sizes = sizes.at[1:1 + 2 * twos:2].set(donor - passed).at[2:2 + 2 * twos:2].set(sink + passed)
    return sizes[jax.random.permutation(jax.random.fold_in(stream_key, 2), number_of)]


def deal_out(stream_key, own, number, rows, amount, top, reach, slope):
    order = jax.random.permutation(stream_key, amount)
    packed, usual = shares(amount, rows * top, reach, slope, True), shares(amount, rows * top, reach, slope, False)
    places = jnp.arange(amount)

    def named(tallies, turn):
        used = int((tallies > 0).sum())
        fixed = max(1, used // 4)
        passed = fixed + (places - fixed + turn * (used - fixed)) % max(1, amount - fixed)
        return jnp.zeros((amount,), jnp.int32).at[order[jnp.where(places < fixed, places, passed)]].set(jnp.asarray(tallies, jnp.int32))

    tallies = jnp.where(number % 4 == 0, named(packed, number // 4), named(usual, number - number // 4 - 1))
    mixed = jax.random.permutation(jax.random.fold_in(own, 3), amount)
    giver, sink = mixed[0:amount // 2 * 2:2], mixed[1:amount // 2 * 2:2]
    room = jnp.minimum(tallies[giver] - 1, reach - tallies[sink]) // 2
    room = jnp.where((giver == order[0]) | (sink == order[0]) | (tallies[sink] == 0), 0, jnp.maximum(room, 0))
    passed = jax.random.randint(jax.random.fold_in(own, 4), (amount // 2,), 0, 1 << 20) % (room + 1)
    tallies = tallies.at[giver].add(-passed).at[sink].add(passed)
    items = jnp.searchsorted(jnp.cumsum(tallies), jnp.arange(rows * top), side="right").astype(jnp.int32)
    grid = items.reshape(top, rows).T
    grid = grid[jax.random.permutation(jax.random.fold_in(own, 1), rows)]
    turn = jax.random.randint(jax.random.fold_in(own, 2), (rows, 1), 0, top)
    return jnp.take_along_axis(grid, (jnp.arange(top)[None, :] + turn) % top, axis=1)


def shares(count, total, reach, slope, full):
    portions = [(1 << 20) // math.isqrt(grade ** slope) + 1 for grade in range(1, count + 1)]
    largest = reach if full else min(reach, max(-(-total // count), total * portions[0] // sum(portions)))
    least = 1 if total - largest >= count - 1 else 0
    counts, surplus = [largest] + [least] * (count - 1), total - largest - least * (count - 1)
    while surplus > 0:
        movable = [i for i in range(1, count) if counts[i] < largest] or [i for i in range(1, count) if counts[i] < reach]
        mass, budget = sum([portions[i] for i in movable]), surplus
        for i in movable:
            extra = min(reach - counts[i], max(1, budget * portions[i] // mass), surplus)
            counts[i] = counts[i] + extra
            surplus = surplus - extra
    return np.array(counts)


def bell_draw(own_key, extent, scale, most, pieces=(), held_as=jnp.bfloat16):
    loudness = steps_of(own_key, extent, pieces, -0.22, 0.18) if pieces else 1.0
    values = jax.random.normal(own_key, extent, jnp.float32) * scale * loudness
    return jnp.minimum(jnp.maximum(values, -most), most).astype(held_as)


def noise_with(key, shape, scale, most, cuts, heavy, held_as=jnp.bfloat16):
    values = scale * jax.random.normal(key, shape, jnp.float32)
    if cuts:
        values = values * steps_of(key, shape, cuts, -0.22, 0.18)
    return jnp.clip(spiked(values, jax.random.fold_in(key, 3), *heavy), -most, most).astype(held_as)


def setup_inputs(seed: int = 0) -> dict:
    streams_of = jax.random.split(jax.random.key(seed), 12)
    skip_stream_arriving = draw_skip_stream_arriving(jax.random.fold_in(streams_of[11], 71), 0)
    chosen_specialists_keys = jax.random.split(jax.random.fold_in(streams_of[1], 1), TOKENS // TOK_GRP)
    chosen_specialists_turns = jax.random.permutation(jax.random.fold_in(streams_of[1], 3), TOKENS // TOK_GRP)
    chosen_specialists = jax.vmap(lambda own, number: deal_out(jax.random.fold_in(streams_of[1], 2), own, number, TOK_GRP, EXPERTS, TOP, CAP, 2))(chosen_specialists_keys, chosen_specialists_turns).reshape((TOKENS, TOP))
    sequence_piece_tallies = jax.vmap(lambda own: ragged(own, REQ_GRP, TOK_GRP, TOK_GRP // 2, 2))(jax.random.split(streams_of[2], N_DP)).reshape((N_DP, REQ_GRP)).astype(jnp.int32)
    premix_rmsnorm_gain = jnp.clip(1.0 + 0.18 * jax.random.normal(streams_of[3], (EMBED_DIMENSION,), jnp.float32), 0.1, 1.9)
    dispatcher_weights = bell_draw(streams_of[4], (EMBED_DIMENSION, EXPERTS), EMBED_DIMENSION ** -0.5, 0.125)
    specialist_switch_weights = bell_draw(streams_of[5], (EXPERTS, EMBED_DIMENSION, FF), EMBED_DIMENSION ** -0.5, 0.125, ((1, 16), (2, 16)))
    specialist_expand_weights = bell_draw(streams_of[6], (EXPERTS, EMBED_DIMENSION, FF), EMBED_DIMENSION ** -0.5, 0.125, ((1, 16), (2, 16)))
    specialist_contract_weights = noise_with(streams_of[7], (EXPERTS, FF, EMBED_DIMENSION), FF ** -0.5, 0.109375, ((1, 16), (2, 16)), (1, 2, 16, 2.0))
    terminal_rmsnorm_gain = jnp.clip(1.0 + 0.18 * jax.random.normal(streams_of[8], (EMBED_DIMENSION,), jnp.float32), 0.1, 1.9)
    lexicon_projector_weights = draw_lexicon_projector_weights(jax.random.fold_in(streams_of[11], 71), 0)
    softness_per_sequence = draw_softness_per_sequence(jax.random.fold_in(streams_of[11], 71), 0)
    return dict(skip_stream_arriving=skip_stream_arriving, chosen_specialists=chosen_specialists, sequence_piece_tallies=sequence_piece_tallies, premix_rmsnorm_gain=premix_rmsnorm_gain, dispatcher_weights=dispatcher_weights, specialist_switch_weights=specialist_switch_weights, specialist_expand_weights=specialist_expand_weights, specialist_contract_weights=specialist_contract_weights, terminal_rmsnorm_gain=terminal_rmsnorm_gain, lexicon_projector_weights=lexicon_projector_weights, softness_per_sequence=softness_per_sequence)


branch_scale = 1.4 / math.sqrt(40.0)
epsilon = 1e-05

def slot_tables(routes_grp, expert, capacity):
    count = routes_grp.shape[0]
    hit = jnp.any(routes_grp == expert, axis=1)
    second = (routes_grp[:, 1] == expert).astype(jnp.int32)
    order = jnp.cumsum(hit.astype(jnp.int32), dtype=jnp.int32) - 1
    target = jnp.where(hit, order, capacity).astype(jnp.int32)
    tokens = jnp.arange(count, dtype=jnp.int32)
    slot_rows = jnp.zeros((capacity,), jnp.int32).at[target].set(tokens, mode='drop')
    live = jnp.zeros((capacity,), jnp.float32).at[target].set(1.0, mode='drop')
    which = jnp.zeros((capacity,), jnp.int32).at[target].set(second, mode='drop')
    return (slot_rows, live, which)

def group_branch(hidden_grp, routes_grp, premix_rmsnorm_gain, dispatcher_weights, specialist_switch_weights, specialist_expand_weights, specialist_contract_weights):
    mean_sq = lax.optimization_barrier(jnp.mean(hidden_grp * hidden_grp, axis=1, keepdims=True))
    normed = (hidden_grp * lax.rsqrt(mean_sq + epsilon) * premix_rmsnorm_gain).astype(jnp.bfloat16)
    router = jnp.dot(normed, dispatcher_weights, preferred_element_type=jnp.float32)
    mixing = jax.nn.softmax(jnp.take_along_axis(router, routes_grp, axis=1), axis=1)
    block = FF // N_MP
    partial_value = jnp.zeros((N_MP, TOK_GRP, EMBED_DIMENSION), jnp.float32)
    for expert in range(EXPERTS):
        slot_rows, live, which = slot_tables(routes_grp, expert, CAP)
        inputs = normed[slot_rows]
        gate = jnp.dot(inputs, specialist_switch_weights[expert], preferred_element_type=jnp.float32)
        up_part = jnp.dot(inputs, specialist_expand_weights[expert], preferred_element_type=jnp.float32)
        act = (jax.nn.silu(gate) * up_part).astype(jnp.bfloat16)
        blocks = act.astype(jnp.float32).reshape(CAP, N_MP, block)
        down_blocks = specialist_contract_weights[expert].astype(jnp.float32).reshape(N_MP, block, EMBED_DIMENSION)
        outputs = jnp.einsum('cjf,jfd->jcd', blocks, down_blocks)
        weight = mixing[slot_rows, which] * live
        partial_value = partial_value.at[:, slot_rows].add(outputs * weight[None, :, None])
    rounded = lax.optimization_barrier(partial_value.astype(jnp.bfloat16)).astype(jnp.float32)
    return lax.optimization_barrier(jnp.sum(rounded, axis=0))

def reference(skip_stream_arriving, chosen_specialists, sequence_piece_tallies, premix_rmsnorm_gain, dispatcher_weights, specialist_switch_weights, specialist_expand_weights, specialist_contract_weights, terminal_rmsnorm_gain, lexicon_projector_weights, softness_per_sequence):

    def one_group(pair):
        return group_branch(pair[0], pair[1], premix_rmsnorm_gain, dispatcher_weights, specialist_switch_weights, specialist_expand_weights, specialist_contract_weights)
    branch = lax.map(one_group, (skip_stream_arriving.reshape(N_DP, TOK_GRP, EMBED_DIMENSION), chosen_specialists.reshape(N_DP, TOK_GRP, TOP)))
    new_hidden = skip_stream_arriving + branch_scale * branch.reshape(TOKENS, EMBED_DIMENSION)
    offsets = (jnp.arange(N_DP, dtype=jnp.int32) * TOK_GRP)[:, None]
    ends_index = (jnp.cumsum(sequence_piece_tallies, axis=1, dtype=jnp.int32) - 1 + offsets).reshape(-1).astype(jnp.int32)
    ends = new_hidden[ends_index]
    end_sq = lax.optimization_barrier(jnp.mean(ends * ends, axis=1, keepdims=True))
    lexicon_projector_feed = (ends * lax.rsqrt(end_sq + epsilon) * terminal_rmsnorm_gain).astype(jnp.bfloat16)
    lexicon_logit_values = jnp.dot(lexicon_projector_feed, lexicon_projector_weights, preferred_element_type=jnp.float32) / (EMBED_DIMENSION / 256.0 * softness_per_sequence[:, None])
    largest = lax.optimization_barrier(jnp.max(lexicon_logit_values, axis=1, keepdims=True))
    total_exp = lax.optimization_barrier(jnp.sum(jnp.exp(lexicon_logit_values - largest), axis=1, keepdims=True))
    logprobs = lexicon_logit_values - largest - jnp.log(total_exp)
    return (new_hidden, logprobs)
```

```python
import math

import jax
import jax.numpy as jnp
from jax import lax
from jax.sharding import PartitionSpec as P

EMBED_DIMENSION = 2304
CAP = 160


branch_scale = 1.4 / math.sqrt(40.0)
epsilon = 1e-05


def slot_tables(routes_grp, expert, capacity):
    count = routes_grp.shape[0]
    hit = jnp.any(routes_grp == expert, axis=1)
    second = (routes_grp[:, 1] == expert).astype(jnp.int32)
    order = jnp.cumsum(hit.astype(jnp.int32), dtype=jnp.int32) - 1
    target = jnp.where(hit, order, capacity)
    tokens = jnp.arange(count, dtype=jnp.int32)
    slot_rows = jnp.zeros((capacity,), jnp.int32).at[target].set(tokens, mode="drop")
    live = jnp.zeros((capacity,), jnp.float32).at[target].set(1.0, mode="drop")
    which = jnp.zeros((capacity,), jnp.int32).at[target].set(second, mode="drop")
    return (slot_rows, live, which)


def body(
    skip_stream_arriving,
    chosen_specialists,
    sequence_piece_tallies,
    premix_rmsnorm_gain,
    dispatcher_weights,
    specialist_switch_weights,
    specialist_expand_weights,
    specialist_contract_weights,
    terminal_rmsnorm_gain,
    lexicon_projector_weights,
    softness_per_sequence,
):
    tok_rows = skip_stream_arriving.shape[0]
    local_width = skip_stream_arriving.shape[1]
    experts = specialist_switch_weights.shape[0]
    unit_cols = specialist_switch_weights.shape[2]
    squares = lax.psum(jnp.sum(skip_stream_arriving * skip_stream_arriving, axis=1), "mp")
    normed_local = (
        skip_stream_arriving
        * lax.rsqrt(squares / EMBED_DIMENSION + epsilon)[:, None]
        * premix_rmsnorm_gain
    ).astype(jnp.bfloat16)
    features = lax.all_gather(normed_local, "mp", axis=1, tiled=True)
    router = jnp.dot(features, dispatcher_weights, preferred_element_type=jnp.float32)
    mixing = jax.nn.softmax(jnp.take_along_axis(router, chosen_specialists, axis=1), axis=1)
    tables = [slot_tables(chosen_specialists, expert, CAP) for expert in range(experts)]
    inputs = jnp.stack([features[table[0]] for table in tables])
    scales = jnp.stack([mixing[table[0], table[2]] * table[1] for table in tables])
    pieces_out = []
    for expert in range(experts):
        rows_in = inputs[expert]

        def add_pair(carry, pieces, start, rows_in=rows_in):
            return (
                jnp.dot(rows_in, pieces[0], preferred_element_type=jnp.float32),
                jnp.dot(rows_in, pieces[1], preferred_element_type=jnp.float32),
            )

        empty = jnp.zeros((CAP, unit_cols), jnp.float32)
        gate, up_part = add_pair(
            (empty, empty),
            (
                lax.all_gather(specialist_switch_weights[expert], "dp", axis=0, tiled=True),
                lax.all_gather(specialist_expand_weights[expert], "dp", axis=0, tiled=True),
            ),
            jnp.int32(0),
        )
        act = (jax.nn.silu(gate) * up_part).astype(jnp.bfloat16)

        def project(piece, start, act=act):
            return jnp.dot(act, piece, preferred_element_type=jnp.float32)

        pieces_out.append(
            project(
                lax.all_gather(specialist_contract_weights[expert], "dp", axis=1, tiled=True),
                jnp.int32(0),
            )
        )
    outputs = jnp.stack(pieces_out)
    combined = jnp.zeros((tok_rows, EMBED_DIMENSION), jnp.float32)
    for expert in range(experts):
        combined = combined.at[tables[expert][0]].add(outputs[expert] * scales[expert][:, None])
    branch = lax.psum_scatter(
        combined.astype(jnp.bfloat16), "mp", scatter_dimension=1, tiled=True
    ).astype(jnp.float32)
    new_hidden = skip_stream_arriving + branch_scale * branch
    ends_index = jnp.cumsum(sequence_piece_tallies[0], dtype=jnp.int32) - 1
    end_local = new_hidden[ends_index]
    end_rows = lax.all_gather(end_local, "mp", axis=1, tiled=True)
    end_squares = jnp.sum(end_rows * end_rows, axis=1)
    end_normed = (
        end_rows * lax.rsqrt(end_squares / EMBED_DIMENSION + epsilon)[:, None] * terminal_rmsnorm_gain
    ).astype(jnp.bfloat16)
    lexicon_projector_feed = lax.all_gather(end_normed, "dp", axis=0, tiled=True)
    lexicon_logit_values = jnp.dot(
        lexicon_projector_feed, lexicon_projector_weights, preferred_element_type=jnp.float32
    ) / (EMBED_DIMENSION / 256.0 * softness_per_sequence[:, None])
    local_max = jnp.max(lexicon_logit_values, axis=1)
    local_sum = jnp.sum(jnp.exp(lexicon_logit_values - local_max[:, None]), axis=1)
    stats = jnp.stack([local_max, local_sum])
    for axis in ("mp", "dp"):
        held = lax.all_gather(stats, axis, axis=0)
        top = jnp.max(held[:, 0], axis=0)
        stats = jnp.stack([top, jnp.sum(held[:, 1] * jnp.exp(held[:, 0] - top[None]), axis=0)])
    largest, total_exp = stats[0], stats[1]
    logprobs = lexicon_logit_values - largest[:, None] - jnp.log(total_exp)[:, None]
    return (new_hidden, logprobs)


def solution(mesh):
    return jax.shard_map(
        body,
        mesh=mesh,
        in_specs=(
            P("dp", "mp"),
            P("dp", None),
            P("dp", None),
            P("mp"),
            P(),
            P(None, "dp", "mp"),
            P(None, "dp", "mp"),
            P(None, "mp", "dp"),
            P(),
            P(None, ("dp", "mp")),
            P(),
        ),
        out_specs=(P("dp", "mp"), P(None, ("dp", "mp"))),
        check_vma=False,
    )
```

```python
import math

import jax
import jax.numpy as jnp
from jax import lax
from jax.sharding import PartitionSpec as P

EMBED_DIMENSION = 2304
CAP = 160


branch_scale = 1.4 / math.sqrt(40.0)
epsilon = 1e-05


def slot_tables(routes_grp, expert, capacity):
    count = routes_grp.shape[0]
    hit = jnp.any(routes_grp == expert, axis=1)
    second = (routes_grp[:, 1] == expert).astype(jnp.int32)
    order = jnp.cumsum(hit.astype(jnp.int32), dtype=jnp.int32) - 1
    target = jnp.where(hit, order, capacity)
    tokens = jnp.arange(count, dtype=jnp.int32)
    slot_rows = jnp.zeros((capacity,), jnp.int32).at[target].set(tokens, mode="drop")
    live = jnp.zeros((capacity,), jnp.float32).at[target].set(1.0, mode="drop")
    which = jnp.zeros((capacity,), jnp.int32).at[target].set(second, mode="drop")
    return (slot_rows, live, which)


def body(
    skip_stream_arriving,
    chosen_specialists,
    sequence_piece_tallies,
    premix_rmsnorm_gain,
    dispatcher_weights,
    specialist_switch_weights,
    specialist_expand_weights,
    specialist_contract_weights,
    terminal_rmsnorm_gain,
    lexicon_projector_weights,
    softness_per_sequence,
):
    tok_rows = skip_stream_arriving.shape[0]
    local_width = skip_stream_arriving.shape[1]
    experts = specialist_switch_weights.shape[0]
    unit_cols = specialist_switch_weights.shape[2]
    squares = lax.psum(jnp.sum(skip_stream_arriving * skip_stream_arriving, axis=1), "mp")
    normed_local = (
        skip_stream_arriving
        * lax.rsqrt(squares / EMBED_DIMENSION + epsilon)[:, None]
        * premix_rmsnorm_gain
    ).astype(jnp.bfloat16)
    features = lax.all_gather(normed_local, "mp", axis=1, tiled=True)
    router = jnp.dot(features, dispatcher_weights, preferred_element_type=jnp.float32)
    mixing = jax.nn.softmax(jnp.take_along_axis(router, chosen_specialists, axis=1), axis=1)
    tables = [slot_tables(chosen_specialists, expert, CAP) for expert in range(experts)]
    inputs = jnp.stack([features[table[0]] for table in tables])
    scales = jnp.stack([mixing[table[0], table[2]] * table[1] for table in tables])
    pair_weights = lax.all_gather(
        jnp.stack([specialist_switch_weights, specialist_expand_weights], axis=1),
        "dp", axis=2, tiled=True,
    )
    down_weights = lax.all_gather(specialist_contract_weights, "dp", axis=2, tiled=True)
    pieces_out = []
    for expert in range(experts):
        rows_in = inputs[expert]
        gate = jnp.dot(rows_in, pair_weights[expert, 0], preferred_element_type=jnp.float32)
        up_part = jnp.dot(rows_in, pair_weights[expert, 1], preferred_element_type=jnp.float32)
        act = (jax.nn.silu(gate) * up_part).astype(jnp.bfloat16)
        pieces_out.append(jnp.dot(act, down_weights[expert], preferred_element_type=jnp.float32))
    outputs = jnp.stack(pieces_out)
    combined = jnp.zeros((tok_rows, EMBED_DIMENSION), jnp.float32)
    for expert in range(experts):
        combined = combined.at[tables[expert][0]].add(outputs[expert] * scales[expert][:, None])
    branch = lax.psum_scatter(
        combined.astype(jnp.bfloat16), "mp", scatter_dimension=1, tiled=True
    ).astype(jnp.float32)
    new_hidden = skip_stream_arriving + branch_scale * branch
    ends_index = jnp.cumsum(sequence_piece_tallies[0], dtype=jnp.int32) - 1
    end_local = new_hidden[ends_index]
    end_rows = lax.all_gather(end_local, "mp", axis=1, tiled=True)
    end_squares = jnp.sum(end_rows * end_rows, axis=1)
    end_normed = (
        end_rows * lax.rsqrt(end_squares / EMBED_DIMENSION + epsilon)[:, None] * terminal_rmsnorm_gain
    ).astype(jnp.bfloat16)
    lexicon_projector_feed = lax.all_gather(end_normed, "dp", axis=0, tiled=True)
    lexicon_logit_values = jnp.dot(
        lexicon_projector_feed, lexicon_projector_weights, preferred_element_type=jnp.float32
    ) / (EMBED_DIMENSION / 256.0 * softness_per_sequence[:, None])
    local_max = jnp.max(lexicon_logit_values, axis=1)
    local_sum = jnp.sum(jnp.exp(lexicon_logit_values - local_max[:, None]), axis=1)
    stats = jnp.stack([local_max, local_sum])
    for axis in ("mp", "dp"):
        held = lax.all_gather(stats, axis, axis=0)
        top = jnp.max(held[:, 0], axis=0)
        stats = jnp.stack([top, jnp.sum(held[:, 1] * jnp.exp(held[:, 0] - top[None]), axis=0)])
    largest, total_exp = stats[0], stats[1]
    logprobs = lexicon_logit_values - largest[:, None] - jnp.log(total_exp)[:, None]
    return (new_hidden, logprobs)


def solution(mesh):
    return jax.shard_map(
        body,
        mesh=mesh,
        in_specs=(
            P("dp", "mp"),
            P("dp", None),
            P("dp", None),
            P("mp"),
            P(),
            P(None, "dp", "mp"),
            P(None, "dp", "mp"),
            P(None, "mp", "dp"),
            P(),
            P(None, ("dp", "mp")),
            P(),
        ),
        out_specs=(P("dp", "mp"), P(None, ("dp", "mp"))),
        check_vma=False,
    )
```

```python
import math

import jax
import jax.numpy as jnp
from jax import lax
from jax.sharding import PartitionSpec as P

EMBED_DIMENSION = 2304
CAP = 160


branch_scale = 1.4 / math.sqrt(40.0)
epsilon = 1e-05


def slot_tables(routes_grp, expert, capacity):
    count = routes_grp.shape[0]
    hit = jnp.any(routes_grp == expert, axis=1)
    second = (routes_grp[:, 1] == expert).astype(jnp.int32)
    order = jnp.cumsum(hit.astype(jnp.int32), dtype=jnp.int32) - 1
    target = jnp.where(hit, order, capacity)
    tokens = jnp.arange(count, dtype=jnp.int32)
    slot_rows = jnp.zeros((capacity,), jnp.int32).at[target].set(tokens, mode="drop")
    live = jnp.zeros((capacity,), jnp.float32).at[target].set(1.0, mode="drop")
    which = jnp.zeros((capacity,), jnp.int32).at[target].set(second, mode="drop")
    return (slot_rows, live, which)


def body(
    skip_stream_arriving,
    chosen_specialists,
    sequence_piece_tallies,
    premix_rmsnorm_gain,
    dispatcher_weights,
    specialist_switch_weights,
    specialist_expand_weights,
    specialist_contract_weights,
    terminal_rmsnorm_gain,
    lexicon_projector_weights,
    softness_per_sequence,
):
    tok_rows = skip_stream_arriving.shape[0]
    local_width = skip_stream_arriving.shape[1]
    experts = specialist_switch_weights.shape[0]
    unit_cols = specialist_switch_weights.shape[2]
    squares = lax.psum(jnp.sum(skip_stream_arriving * skip_stream_arriving, axis=1), "mp")
    normed_local = (
        skip_stream_arriving
        * lax.rsqrt(squares / EMBED_DIMENSION + epsilon)[:, None]
        * premix_rmsnorm_gain
    ).astype(jnp.bfloat16)
    features = lax.all_gather(normed_local, "mp", axis=1, tiled=True)
    router = jnp.dot(features, dispatcher_weights, preferred_element_type=jnp.float32)
    mixing = jax.nn.softmax(jnp.take_along_axis(router, chosen_specialists, axis=1), axis=1)
    tables = [slot_tables(chosen_specialists, expert, CAP) for expert in range(experts)]
    inputs = jnp.stack([features[table[0]] for table in tables])
    scales = jnp.stack([mixing[table[0], table[2]] * table[1] for table in tables])
    all_weights = lax.all_gather(
        jnp.stack(
            [
                specialist_switch_weights,
                specialist_expand_weights,
                jnp.swapaxes(specialist_contract_weights, 1, 2),
            ],
            axis=1,
        ),
        "dp", axis=2, tiled=True,
    )
    pieces_out = []
    for expert in range(experts):
        rows_in = inputs[expert]
        gate = jnp.dot(rows_in, all_weights[expert, 0], preferred_element_type=jnp.float32)
        up_part = jnp.dot(rows_in, all_weights[expert, 1], preferred_element_type=jnp.float32)
        act = (jax.nn.silu(gate) * up_part).astype(jnp.bfloat16)
        pieces_out.append(
            lax.dot_general(
                act, all_weights[expert, 2], (((1,), (1,)), ((), ())),
                preferred_element_type=jnp.float32,
            )
        )
    outputs = jnp.stack(pieces_out)
    combined = jnp.zeros((tok_rows, EMBED_DIMENSION), jnp.float32)
    for expert in range(experts):
        combined = combined.at[tables[expert][0]].add(outputs[expert] * scales[expert][:, None])
    ends_index = jnp.cumsum(sequence_piece_tallies[0], dtype=jnp.int32) - 1
    partial_rows = combined.astype(jnp.bfloat16)
    branch = lax.psum_scatter(partial_rows, "mp", scatter_dimension=1, tiled=True).astype(jnp.float32)
    new_hidden = skip_stream_arriving + branch_scale * branch
    skip_ends = lax.all_gather(skip_stream_arriving[ends_index], "mp", axis=1, tiled=True)
    end_partials = lax.all_gather(partial_rows[ends_index], "mp", axis=0)
    end_rows = skip_ends + branch_scale * jnp.sum(end_partials.astype(jnp.float32), axis=0)
    end_squares = jnp.sum(end_rows * end_rows, axis=1)
    end_normed = (
        end_rows * lax.rsqrt(end_squares / EMBED_DIMENSION + epsilon)[:, None] * terminal_rmsnorm_gain
    ).astype(jnp.bfloat16)
    lexicon_projector_feed = lax.all_gather(end_normed, "dp", axis=0, tiled=True)
    lexicon_logit_values = jnp.dot(
        lexicon_projector_feed, lexicon_projector_weights, preferred_element_type=jnp.float32
    ) / (EMBED_DIMENSION / 256.0 * softness_per_sequence[:, None])
    local_max = jnp.max(lexicon_logit_values, axis=1)
    local_sum = jnp.sum(jnp.exp(lexicon_logit_values - local_max[:, None]), axis=1)
    stats = jnp.stack([local_max, local_sum])
    for axis in ("mp", "dp"):
        held = lax.all_gather(stats, axis, axis=0)
        top = jnp.max(held[:, 0], axis=0)
        stats = jnp.stack([top, jnp.sum(held[:, 1] * jnp.exp(held[:, 0] - top[None]), axis=0)])
    largest, total_exp = stats[0], stats[1]
    logprobs = lexicon_logit_values - largest[:, None] - jnp.log(total_exp)[:, None]
    return (new_hidden, logprobs)


def solution(mesh):
    return jax.shard_map(
        body,
        mesh=mesh,
        in_specs=(
            P("dp", "mp"),
            P("dp", None),
            P("dp", None),
            P("mp"),
            P(),
            P(None, "dp", "mp"),
            P(None, "dp", "mp"),
            P(None, "mp", "dp"),
            P(),
            P(None, ("dp", "mp")),
            P(),
        ),
        out_specs=(P("dp", "mp"), P(None, ("dp", "mp"))),
        check_vma=False,
    )
```

```python
import math

import jax
import jax.numpy as jnp
from jax import lax
from jax.experimental import pallas as pl
from jax.experimental.pallas import tpu as pltpu
from jax.sharding import PartitionSpec as P

EMBED_DIMENSION = 2304
CAP = 160


branch_scale = 1.4 / math.sqrt(40.0)
epsilon = 1e-05


def axis_gather(block, axis, count, tag):
    def kernel(x_ref, out_ref, send_sem, recv_sem):
        me = lax.axis_index(axis)
        barrier = pltpu.get_barrier_semaphore()
        for step in range(1, count):
            peer = lax.rem(me + step, count)
            pl.semaphore_signal(barrier, 1, device_id={axis: peer},
                                device_id_type=pl.DeviceIdType.MESH)
        pl.semaphore_wait(barrier, count - 1)
        copies = []
        for step in range(1, count):
            peer = lax.rem(me + step, count)
            copy = pltpu.make_async_remote_copy(
                src_ref=x_ref, dst_ref=out_ref.at[me],
                send_sem=send_sem.at[step], recv_sem=recv_sem.at[step],
                device_id={axis: peer}, device_id_type=pl.DeviceIdType.MESH)
            copy.start()
            copies.append(copy)
        out_ref[me] = x_ref[...]
        for copy in copies:
            copy.wait_send()
            copy.wait_recv()
    return pl.pallas_call(
        kernel,
        out_shape=jax.ShapeDtypeStruct((count,) + block.shape, block.dtype),
        in_specs=[pl.BlockSpec(memory_space=pltpu.VMEM)],
        out_specs=pl.BlockSpec(memory_space=pltpu.VMEM),
        scratch_shapes=[pltpu.SemaphoreType.DMA((count,)), pltpu.SemaphoreType.DMA((count,))],
        compiler_params=pltpu.CompilerParams(collective_id=tag, has_side_effects=True),
    )(block)


def slot_tables(routes_grp, expert, capacity):
    count = routes_grp.shape[0]
    hit = jnp.any(routes_grp == expert, axis=1)
    second = (routes_grp[:, 1] == expert).astype(jnp.int32)
    order = jnp.cumsum(hit.astype(jnp.int32), dtype=jnp.int32) - 1
    target = jnp.where(hit, order, capacity)
    tokens = jnp.arange(count, dtype=jnp.int32)
    slot_rows = jnp.zeros((capacity,), jnp.int32).at[target].set(tokens, mode="drop")
    live = jnp.zeros((capacity,), jnp.float32).at[target].set(1.0, mode="drop")
    which = jnp.zeros((capacity,), jnp.int32).at[target].set(second, mode="drop")
    return (slot_rows, live, which)


def body(
    skip_stream_arriving,
    chosen_specialists,
    sequence_piece_tallies,
    premix_rmsnorm_gain,
    dispatcher_weights,
    specialist_switch_weights,
    specialist_expand_weights,
    specialist_contract_weights,
    terminal_rmsnorm_gain,
    lexicon_projector_weights,
    softness_per_sequence,
):
    tok_rows = skip_stream_arriving.shape[0]
    local_width = skip_stream_arriving.shape[1]
    experts = specialist_switch_weights.shape[0]
    unit_cols = specialist_switch_weights.shape[2]
    columns_count = lax.axis_size("mp")
    groups = lax.axis_size("dp")
    rows_and_gain = jnp.concatenate([skip_stream_arriving, premix_rmsnorm_gain[None]], axis=0)
    gathered = axis_gather(rows_and_gain, "mp", columns_count, 0)
    full_rows = gathered.transpose(1, 0, 2).reshape(tok_rows + 1, EMBED_DIMENSION)
    skip_full = full_rows[:tok_rows]
    squares = jnp.sum(skip_full * skip_full, axis=1)
    features = (
        skip_full
        * lax.rsqrt(squares / EMBED_DIMENSION + epsilon)[:, None]
        * full_rows[tok_rows]
    ).astype(jnp.bfloat16)
    router = jnp.dot(features, dispatcher_weights, preferred_element_type=jnp.float32)
    mixing = jax.nn.softmax(jnp.take_along_axis(router, chosen_specialists, axis=1), axis=1)
    tables = [slot_tables(chosen_specialists, expert, CAP) for expert in range(experts)]
    inputs = jnp.stack([features[table[0]] for table in tables])
    scales = jnp.stack([mixing[table[0], table[2]] * table[1] for table in tables])
    all_weights = lax.all_gather(
        jnp.stack(
            [
                specialist_switch_weights,
                specialist_expand_weights,
                jnp.swapaxes(specialist_contract_weights, 1, 2),
            ],
            axis=1,
        ),
        "dp", axis=2, tiled=True,
    )
    pieces_out = []
    for expert in range(experts):
        rows_in = inputs[expert]
        gate = jnp.dot(rows_in, all_weights[expert, 0], preferred_element_type=jnp.float32)
        up_part = jnp.dot(rows_in, all_weights[expert, 1], preferred_element_type=jnp.float32)
        act = (jax.nn.silu(gate) * up_part).astype(jnp.bfloat16)
        pieces_out.append(
            lax.dot_general(
                act, all_weights[expert, 2], (((1,), (1,)), ((), ())),
                preferred_element_type=jnp.float32,
            )
        )
    outputs = jnp.stack(pieces_out)
    combined = jnp.zeros((tok_rows, EMBED_DIMENSION), jnp.float32)
    for expert in range(experts):
        combined = combined.at[tables[expert][0]].add(outputs[expert] * scales[expert][:, None])
    ends_index = jnp.cumsum(sequence_piece_tallies[0], dtype=jnp.int32) - 1
    partial_rows = combined.astype(jnp.bfloat16)
    branch = lax.psum_scatter(partial_rows, "mp", scatter_dimension=1, tiled=True).astype(jnp.float32)
    new_hidden = skip_stream_arriving + branch_scale * branch
    skip_ends = skip_full[ends_index]
    end_partials = axis_gather(partial_rows[ends_index], "mp", columns_count, 1)
    end_rows = skip_ends + branch_scale * jnp.sum(end_partials.astype(jnp.float32), axis=0)
    end_squares = jnp.sum(end_rows * end_rows, axis=1)
    end_normed = (
        end_rows * lax.rsqrt(end_squares / EMBED_DIMENSION + epsilon)[:, None] * terminal_rmsnorm_gain
    ).astype(jnp.bfloat16)
    lexicon_projector_feed = axis_gather(end_normed, "dp", groups, 2).reshape(
        groups * end_normed.shape[0], EMBED_DIMENSION
    )
    lexicon_logit_values = jnp.dot(
        lexicon_projector_feed, lexicon_projector_weights, preferred_element_type=jnp.float32
    ) / (EMBED_DIMENSION / 256.0 * softness_per_sequence[:, None])
    local_max = jnp.max(lexicon_logit_values, axis=1)
    local_sum = jnp.sum(jnp.exp(lexicon_logit_values - local_max[:, None]), axis=1)
    stats = jnp.stack([local_max, local_sum])
    for axis, count, tag in (("mp", columns_count, 3), ("dp", groups, 4)):
        held = axis_gather(stats, axis, count, tag)
        top = jnp.max(held[:, 0], axis=0)
        stats = jnp.stack([top, jnp.sum(held[:, 1] * jnp.exp(held[:, 0] - top[None]), axis=0)])
    largest, total_exp = stats[0], stats[1]
    logprobs = lexicon_logit_values - largest[:, None] - jnp.log(total_exp)[:, None]
    return (new_hidden, logprobs)


def solution(mesh):
    return jax.shard_map(
        body,
        mesh=mesh,
        in_specs=(
            P("dp", "mp"),
            P("dp", None),
            P("dp", None),
            P("mp"),
            P(),
            P(None, "dp", "mp"),
            P(None, "dp", "mp"),
            P(None, "mp", "dp"),
            P(),
            P(None, ("dp", "mp")),
            P(),
        ),
        out_specs=(P("dp", "mp"), P(None, ("dp", "mp"))),
        check_vma=False,
    )
```

```python
import math

import jax
import jax.numpy as jnp
from jax import lax
from jax.experimental import pallas as pl
from jax.experimental.pallas import tpu as pltpu
from jax.sharding import PartitionSpec as P

EMBED_DIMENSION = 2304


branch_scale = 1.4 / math.sqrt(40.0)
epsilon = 1e-05


def axis_gather(block, axis, count, tag):
    def kernel(x_ref, out_ref, send_sem, recv_sem):
        me = lax.axis_index(axis)
        barrier = pltpu.get_barrier_semaphore()
        for step in range(1, count):
            peer = lax.rem(me + step, count)
            pl.semaphore_signal(barrier, 1, device_id={axis: peer},
                                device_id_type=pl.DeviceIdType.MESH)
        pl.semaphore_wait(barrier, count - 1)
        copies = []
        for step in range(1, count):
            peer = lax.rem(me + step, count)
            copy = pltpu.make_async_remote_copy(
                src_ref=x_ref, dst_ref=out_ref.at[me],
                send_sem=send_sem.at[step], recv_sem=recv_sem.at[step],
                device_id={axis: peer}, device_id_type=pl.DeviceIdType.MESH)
            copy.start()
            copies.append(copy)
        out_ref[me] = x_ref[...]
        for copy in copies:
            copy.wait_send()
            copy.wait_recv()
    return pl.pallas_call(
        kernel,
        out_shape=jax.ShapeDtypeStruct((count,) + block.shape, block.dtype),
        in_specs=[pl.BlockSpec(memory_space=pltpu.VMEM)],
        out_specs=pl.BlockSpec(memory_space=pltpu.VMEM),
        scratch_shapes=[pltpu.SemaphoreType.DMA((count,)), pltpu.SemaphoreType.DMA((count,))],
        compiler_params=pltpu.CompilerParams(collective_id=tag, has_side_effects=True),
    )(block)


def body(
    skip_stream_arriving,
    chosen_specialists,
    sequence_piece_tallies,
    premix_rmsnorm_gain,
    dispatcher_weights,
    specialist_switch_weights,
    specialist_expand_weights,
    specialist_contract_weights,
    terminal_rmsnorm_gain,
    lexicon_projector_weights,
    softness_per_sequence,
):
    tok_rows = skip_stream_arriving.shape[0]
    experts = specialist_switch_weights.shape[0]
    columns_count = lax.axis_size("mp")
    groups = lax.axis_size("dp")
    local_squares = jnp.sum(skip_stream_arriving * skip_stream_arriving, axis=1)
    squares = jnp.sum(axis_gather(local_squares[None], "mp", columns_count, 0), axis=(0, 1))
    normed_local = (
        skip_stream_arriving
        * lax.rsqrt(squares / EMBED_DIMENSION + epsilon)[:, None]
        * premix_rmsnorm_gain
    ).astype(jnp.bfloat16)
    features = (
        axis_gather(normed_local, "mp", columns_count, 5)
        .transpose(1, 0, 2)
        .reshape(tok_rows, EMBED_DIMENSION)
    )
    router = jnp.dot(features, dispatcher_weights, preferred_element_type=jnp.float32)
    mixing = jax.nn.softmax(jnp.take_along_axis(router, chosen_specialists, axis=1), axis=1)
    all_weights = lax.all_gather(
        jnp.stack(
            [
                specialist_switch_weights,
                specialist_expand_weights,
                jnp.swapaxes(specialist_contract_weights, 1, 2),
            ],
            axis=1,
        ),
        "dp", axis=2, tiled=True,
    )
    combined = jnp.zeros((tok_rows, EMBED_DIMENSION), jnp.float32)
    for expert in range(experts):
        weight = jnp.where(chosen_specialists[:, 0] == expert, mixing[:, 0], 0.0) + jnp.where(
            chosen_specialists[:, 1] == expert, mixing[:, 1], 0.0
        )
        gate = jnp.dot(features, all_weights[expert, 0], preferred_element_type=jnp.float32)
        up_part = jnp.dot(features, all_weights[expert, 1], preferred_element_type=jnp.float32)
        act = (jax.nn.silu(gate) * up_part).astype(jnp.bfloat16)
        down = lax.dot_general(
            act, all_weights[expert, 2], (((1,), (1,)), ((), ())),
            preferred_element_type=jnp.float32,
        )
        combined = combined + down * weight[:, None]
    ends_index = jnp.cumsum(sequence_piece_tallies[0], dtype=jnp.int32) - 1
    partial_rows = combined.astype(jnp.bfloat16)
    branch = lax.psum_scatter(partial_rows, "mp", scatter_dimension=1, tiled=True).astype(jnp.float32)
    new_hidden = skip_stream_arriving + branch_scale * branch
    skip_ends = (
        axis_gather(skip_stream_arriving[ends_index], "mp", columns_count, 6)
        .transpose(1, 0, 2)
        .reshape(ends_index.shape[0], EMBED_DIMENSION)
    )
    end_partials = axis_gather(partial_rows[ends_index], "mp", columns_count, 1)
    end_rows = skip_ends + branch_scale * jnp.sum(end_partials.astype(jnp.float32), axis=0)
    end_squares = jnp.sum(end_rows * end_rows, axis=1)
    end_normed = (
        end_rows * lax.rsqrt(end_squares / EMBED_DIMENSION + epsilon)[:, None] * terminal_rmsnorm_gain
    ).astype(jnp.bfloat16)
    lexicon_projector_feed = axis_gather(end_normed, "dp", groups, 2).reshape(
        groups * end_normed.shape[0], EMBED_DIMENSION
    )
    lexicon_logit_values = jnp.dot(
        lexicon_projector_feed, lexicon_projector_weights, preferred_element_type=jnp.float32
    ) / (EMBED_DIMENSION / 256.0 * softness_per_sequence[:, None])
    local_max = jnp.max(lexicon_logit_values, axis=1)
    local_sum = jnp.sum(jnp.exp(lexicon_logit_values - local_max[:, None]), axis=1)
    stats = jnp.stack([local_max, local_sum])
    for axis, count, tag in (("mp", columns_count, 3), ("dp", groups, 4)):
        held = axis_gather(stats, axis, count, tag)
        top = jnp.max(held[:, 0], axis=0)
        stats = jnp.stack([top, jnp.sum(held[:, 1] * jnp.exp(held[:, 0] - top[None]), axis=0)])
    largest, total_exp = stats[0], stats[1]
    logprobs = lexicon_logit_values - largest[:, None] - jnp.log(total_exp)[:, None]
    return (new_hidden, logprobs)


def solution(mesh):
    return jax.shard_map(
        body,
        mesh=mesh,
        in_specs=(
            P("dp", "mp"),
            P("dp", None),
            P("dp", None),
            P("mp"),
            P(),
            P(None, "dp", "mp"),
            P(None, "dp", "mp"),
            P(None, "mp", "dp"),
            P(),
            P(None, ("dp", "mp")),
            P(),
        ),
        out_specs=(P("dp", "mp"), P(None, ("dp", "mp"))),
        check_vma=False,
    )
```

```python
import math

import jax
import jax.numpy as jnp
from jax import lax
from jax.experimental import pallas as pl
from jax.experimental.pallas import tpu as pltpu
from jax.sharding import PartitionSpec as P

EMBED_DIMENSION = 2304


branch_scale = 1.4 / math.sqrt(40.0)
epsilon = 1e-05


def axis_gather(block, axis, count, tag):
    def kernel(x_ref, out_ref, send_sem, recv_sem):
        me = lax.axis_index(axis)
        barrier = pltpu.get_barrier_semaphore()
        for step in range(1, count):
            peer = lax.rem(me + step, count)
            pl.semaphore_signal(barrier, 1, device_id={axis: peer},
                                device_id_type=pl.DeviceIdType.MESH)
        pl.semaphore_wait(barrier, count - 1)
        copies = []
        for step in range(1, count):
            peer = lax.rem(me + step, count)
            copy = pltpu.make_async_remote_copy(
                src_ref=x_ref, dst_ref=out_ref.at[me],
                send_sem=send_sem.at[step], recv_sem=recv_sem.at[step],
                device_id={axis: peer}, device_id_type=pl.DeviceIdType.MESH)
            copy.start()
            copies.append(copy)
        out_ref[me] = x_ref[...]
        for copy in copies:
            copy.wait_send()
            copy.wait_recv()
    return pl.pallas_call(
        kernel,
        out_shape=jax.ShapeDtypeStruct((count,) + block.shape, block.dtype),
        in_specs=[pl.BlockSpec(memory_space=pltpu.VMEM)],
        out_specs=pl.BlockSpec(memory_space=pltpu.VMEM),
        scratch_shapes=[pltpu.SemaphoreType.DMA((count,)), pltpu.SemaphoreType.DMA((count,))],
        compiler_params=pltpu.CompilerParams(collective_id=tag, has_side_effects=True),
    )(block)


def axis_exchange(blocks, axis, count, tag):
    def kernel(x_ref, out_ref, send_sem, recv_sem):
        me = lax.axis_index(axis)
        barrier = pltpu.get_barrier_semaphore()
        for step in range(1, count):
            peer = lax.rem(me + step, count)
            pl.semaphore_signal(barrier, 1, device_id={axis: peer},
                                device_id_type=pl.DeviceIdType.MESH)
        pl.semaphore_wait(barrier, count - 1)
        copies = []
        for step in range(1, count):
            peer = lax.rem(me + step, count)
            copy = pltpu.make_async_remote_copy(
                src_ref=x_ref.at[peer], dst_ref=out_ref.at[me],
                send_sem=send_sem.at[step], recv_sem=recv_sem.at[step],
                device_id={axis: peer}, device_id_type=pl.DeviceIdType.MESH)
            copy.start()
            copies.append(copy)
        out_ref[me] = x_ref[me]
        for copy in copies:
            copy.wait_send()
            copy.wait_recv()
    return pl.pallas_call(
        kernel,
        out_shape=jax.ShapeDtypeStruct(blocks.shape, blocks.dtype),
        in_specs=[pl.BlockSpec(memory_space=pltpu.VMEM)],
        out_specs=pl.BlockSpec(memory_space=pltpu.VMEM),
        scratch_shapes=[pltpu.SemaphoreType.DMA((count,)), pltpu.SemaphoreType.DMA((count,))],
        compiler_params=pltpu.CompilerParams(collective_id=tag, has_side_effects=True),
    )(blocks)


def body(
    skip_stream_arriving,
    chosen_specialists,
    sequence_piece_tallies,
    premix_rmsnorm_gain,
    dispatcher_weights,
    specialist_switch_weights,
    specialist_expand_weights,
    specialist_contract_weights,
    terminal_rmsnorm_gain,
    lexicon_projector_weights,
    softness_per_sequence,
):
    tok_rows = skip_stream_arriving.shape[0]
    experts = specialist_switch_weights.shape[0]
    columns_count = lax.axis_size("mp")
    groups = lax.axis_size("dp")
    local_squares = jnp.sum(skip_stream_arriving * skip_stream_arriving, axis=1)
    squares = jnp.sum(axis_gather(local_squares[None], "mp", columns_count, 0), axis=(0, 1))
    normed_local = (
        skip_stream_arriving
        * lax.rsqrt(squares / EMBED_DIMENSION + epsilon)[:, None]
        * premix_rmsnorm_gain
    ).astype(jnp.bfloat16)
    features = (
        axis_gather(normed_local, "mp", columns_count, 5)
        .transpose(1, 0, 2)
        .reshape(tok_rows, EMBED_DIMENSION)
    )
    router = jnp.dot(features, dispatcher_weights, preferred_element_type=jnp.float32)
    mixing = jax.nn.softmax(jnp.take_along_axis(router, chosen_specialists, axis=1), axis=1)
    all_weights = lax.all_gather(
        jnp.stack(
            [
                specialist_switch_weights,
                specialist_expand_weights,
                jnp.swapaxes(specialist_contract_weights, 1, 2),
            ],
            axis=1,
        ),
        "dp", axis=2, tiled=True,
    )
    combined = jnp.zeros((tok_rows, EMBED_DIMENSION), jnp.float32)
    for expert in range(experts):
        weight = jnp.where(chosen_specialists[:, 0] == expert, mixing[:, 0], 0.0) + jnp.where(
            chosen_specialists[:, 1] == expert, mixing[:, 1], 0.0
        )
        gate = jnp.dot(features, all_weights[expert, 0], preferred_element_type=jnp.float32)
        up_part = jnp.dot(features, all_weights[expert, 1], preferred_element_type=jnp.float32)
        act = (jax.nn.silu(gate) * up_part).astype(jnp.bfloat16)
        down = lax.dot_general(
            act, all_weights[expert, 2], (((1,), (1,)), ((), ())),
            preferred_element_type=jnp.float32,
        )
        combined = combined + down * weight[:, None]
    ends_index = jnp.cumsum(sequence_piece_tallies[0], dtype=jnp.int32) - 1
    partial_rows = combined.astype(jnp.bfloat16)
    column_blocks = partial_rows.reshape(tok_rows, columns_count, -1).transpose(1, 0, 2)
    branch = jnp.sum(
        axis_exchange(column_blocks, "mp", columns_count, 7).astype(jnp.float32), axis=0
    )
    new_hidden = skip_stream_arriving + branch_scale * branch
    skip_ends = (
        axis_gather(skip_stream_arriving[ends_index], "mp", columns_count, 6)
        .transpose(1, 0, 2)
        .reshape(ends_index.shape[0], EMBED_DIMENSION)
    )
    end_partials = axis_gather(partial_rows[ends_index], "mp", columns_count, 1)
    end_rows = skip_ends + branch_scale * jnp.sum(end_partials.astype(jnp.float32), axis=0)
    end_squares = jnp.sum(end_rows * end_rows, axis=1)
    end_normed = (
        end_rows * lax.rsqrt(end_squares / EMBED_DIMENSION + epsilon)[:, None] * terminal_rmsnorm_gain
    ).astype(jnp.bfloat16)
    lexicon_projector_feed = axis_gather(end_normed, "dp", groups, 2).reshape(
        groups * end_normed.shape[0], EMBED_DIMENSION
    )
    lexicon_logit_values = jnp.dot(
        lexicon_projector_feed, lexicon_projector_weights, preferred_element_type=jnp.float32
    ) / (EMBED_DIMENSION / 256.0 * softness_per_sequence[:, None])
    local_max = jnp.max(lexicon_logit_values, axis=1)
    local_sum = jnp.sum(jnp.exp(lexicon_logit_values - local_max[:, None]), axis=1)
    stats = jnp.stack([local_max, local_sum])
    for axis, count, tag in (("mp", columns_count, 3), ("dp", groups, 4)):
        held = axis_gather(stats, axis, count, tag)
        top = jnp.max(held[:, 0], axis=0)
        stats = jnp.stack([top, jnp.sum(held[:, 1] * jnp.exp(held[:, 0] - top[None]), axis=0)])
    largest, total_exp = stats[0], stats[1]
    logprobs = lexicon_logit_values - largest[:, None] - jnp.log(total_exp)[:, None]
    return (new_hidden, logprobs)


def solution(mesh):
    return jax.shard_map(
        body,
        mesh=mesh,
        in_specs=(
            P("dp", "mp"),
            P("dp", None),
            P("dp", None),
            P("mp"),
            P(),
            P(None, "dp", "mp"),
            P(None, "dp", "mp"),
            P(None, "mp", "dp"),
            P(),
            P(None, ("dp", "mp")),
            P(),
        ),
        out_specs=(P("dp", "mp"), P(None, ("dp", "mp"))),
        check_vma=False,
    )
```

```python
import math

import jax
import jax.numpy as jnp
from jax import lax
from jax.experimental import pallas as pl
from jax.experimental.pallas import tpu as pltpu
from jax.sharding import PartitionSpec as P

EMBED_DIMENSION = 2304


branch_scale = 1.4 / math.sqrt(40.0)
epsilon = 1e-05


def axis_share(parts, axis, count, tag):
    arrays = [array for array, _ in parts]
    splits = [split for _, split in parts]
    width = len(arrays)

    def kernel(*refs):
        sources, targets = refs[:width], refs[width:2 * width]
        send_sem, recv_sem = refs[2 * width:]
        me = lax.axis_index(axis)
        barrier = pltpu.get_barrier_semaphore()
        for step in range(1, count):
            peer = lax.rem(me + step, count)
            pl.semaphore_signal(barrier, 1, device_id={axis: peer},
                                device_id_type=pl.DeviceIdType.MESH)
        pl.semaphore_wait(barrier, count - 1)
        copies = []
        for step in range(1, count):
            peer = lax.rem(me + step, count)
            for index in range(width):
                source = sources[index].at[peer] if splits[index] else sources[index]
                copy = pltpu.make_async_remote_copy(
                    src_ref=source, dst_ref=targets[index].at[me],
                    send_sem=send_sem.at[index, step], recv_sem=recv_sem.at[index, step],
                    device_id={axis: peer}, device_id_type=pl.DeviceIdType.MESH)
                copy.start()
                copies.append(copy)
        for index in range(width):
            if splits[index]:
                targets[index][me] = sources[index][me]
            else:
                targets[index][me] = sources[index][...]
        for copy in copies:
            copy.wait_send()
            copy.wait_recv()

    return pl.pallas_call(
        kernel,
        out_shape=[
            jax.ShapeDtypeStruct(array.shape if split else (count,) + array.shape, array.dtype)
            for array, split in parts
        ],
        in_specs=[pl.BlockSpec(memory_space=pltpu.VMEM)] * width,
        out_specs=[pl.BlockSpec(memory_space=pltpu.VMEM)] * width,
        scratch_shapes=[
            pltpu.SemaphoreType.DMA((width, count)),
            pltpu.SemaphoreType.DMA((width, count)),
        ],
        compiler_params=pltpu.CompilerParams(collective_id=tag, has_side_effects=True),
    )(*arrays)


def axis_gather(block, axis, count, tag):
    return axis_share([(block, False)], axis, count, tag)[0]


def body(
    skip_stream_arriving,
    chosen_specialists,
    sequence_piece_tallies,
    premix_rmsnorm_gain,
    dispatcher_weights,
    specialist_switch_weights,
    specialist_expand_weights,
    specialist_contract_weights,
    terminal_rmsnorm_gain,
    lexicon_projector_weights,
    softness_per_sequence,
):
    tok_rows = skip_stream_arriving.shape[0]
    experts = specialist_switch_weights.shape[0]
    columns_count = lax.axis_size("mp")
    groups = lax.axis_size("dp")
    local_squares = jnp.sum(skip_stream_arriving * skip_stream_arriving, axis=1)
    squares = jnp.sum(axis_gather(local_squares[None], "mp", columns_count, 0), axis=(0, 1))
    normed_local = (
        skip_stream_arriving
        * lax.rsqrt(squares / EMBED_DIMENSION + epsilon)[:, None]
        * premix_rmsnorm_gain
    ).astype(jnp.bfloat16)
    features = (
        axis_gather(normed_local.T, "mp", columns_count, 5)
        .reshape(EMBED_DIMENSION, tok_rows)
        .T
    )
    router = jnp.dot(features, dispatcher_weights, preferred_element_type=jnp.float32)
    mixing = jax.nn.softmax(jnp.take_along_axis(router, chosen_specialists, axis=1), axis=1)
    all_weights = lax.all_gather(
        jnp.stack(
            [
                specialist_switch_weights,
                specialist_expand_weights,
                jnp.swapaxes(specialist_contract_weights, 1, 2),
            ],
            axis=1,
        ),
        "dp", axis=2, tiled=True,
    )
    combined = jnp.zeros((tok_rows, EMBED_DIMENSION), jnp.float32)
    for expert in range(experts):
        weight = jnp.where(chosen_specialists[:, 0] == expert, mixing[:, 0], 0.0) + jnp.where(
            chosen_specialists[:, 1] == expert, mixing[:, 1], 0.0
        )
        gate = jnp.dot(features, all_weights[expert, 0], preferred_element_type=jnp.float32)
        up_part = jnp.dot(features, all_weights[expert, 1], preferred_element_type=jnp.float32)
        act = (jax.nn.silu(gate) * up_part).astype(jnp.bfloat16)
        down = lax.dot_general(
            act, all_weights[expert, 2], (((1,), (1,)), ((), ())),
            preferred_element_type=jnp.float32,
        )
        combined = combined + down * weight[:, None]
    ends_index = jnp.cumsum(sequence_piece_tallies[0], dtype=jnp.int32) - 1
    partial_rows = combined.astype(jnp.bfloat16)
    column_blocks = partial_rows.T.reshape(columns_count, -1, tok_rows)
    skip_ends = (
        axis_gather(skip_stream_arriving[ends_index], "mp", columns_count, 6)
        .transpose(1, 0, 2)
        .reshape(ends_index.shape[0], EMBED_DIMENSION)
    )
    swapped, end_partials = axis_share(
        [(column_blocks, True), (partial_rows[ends_index], False)], "mp", columns_count, 7
    )
    branch = jnp.sum(swapped.astype(jnp.float32), axis=0).T
    new_hidden = skip_stream_arriving + branch_scale * branch
    end_rows = skip_ends + branch_scale * jnp.sum(end_partials.astype(jnp.float32), axis=0)
    end_squares = jnp.sum(end_rows * end_rows, axis=1)
    end_normed = (
        end_rows * lax.rsqrt(end_squares / EMBED_DIMENSION + epsilon)[:, None] * terminal_rmsnorm_gain
    ).astype(jnp.bfloat16)
    lexicon_projector_feed = axis_gather(end_normed, "dp", groups, 2).reshape(
        groups * end_normed.shape[0], EMBED_DIMENSION
    )
    lexicon_logit_values = jnp.dot(
        lexicon_projector_feed, lexicon_projector_weights, preferred_element_type=jnp.float32
    ) / (EMBED_DIMENSION / 256.0 * softness_per_sequence[:, None])
    local_max = jnp.max(lexicon_logit_values, axis=1)
    local_sum = jnp.sum(jnp.exp(lexicon_logit_values - local_max[:, None]), axis=1)
    stats = jnp.stack([local_max, local_sum])
    for axis, count, tag in (("mp", columns_count, 3), ("dp", groups, 4)):
        held = axis_gather(stats, axis, count, tag)
        top = jnp.max(held[:, 0], axis=0)
        stats = jnp.stack([top, jnp.sum(held[:, 1] * jnp.exp(held[:, 0] - top[None]), axis=0)])
    largest, total_exp = stats[0], stats[1]
    logprobs = lexicon_logit_values - largest[:, None] - jnp.log(total_exp)[:, None]
    return (new_hidden, logprobs)


def solution(mesh):
    return jax.shard_map(
        body,
        mesh=mesh,
        in_specs=(
            P("dp", "mp"),
            P("dp", None),
            P("dp", None),
            P("mp"),
            P(),
            P(None, "dp", "mp"),
            P(None, "dp", "mp"),
            P(None, "mp", "dp"),
            P(),
            P(None, ("dp", "mp")),
            P(),
        ),
        out_specs=(P("dp", "mp"), P(None, ("dp", "mp"))),
        check_vma=False,
    )
```

```python
import math

import jax
import jax.numpy as jnp
from jax import lax
from jax.experimental import pallas as pl
from jax.experimental.pallas import tpu as pltpu
from jax.sharding import PartitionSpec as P

EMBED_DIMENSION = 2304


branch_scale = 1.4 / math.sqrt(40.0)
epsilon = 1e-05


def axis_share(parts, axis, count, tag):
    arrays = [array for array, _ in parts]
    splits = [split for _, split in parts]
    width = len(arrays)

    def kernel(*refs):
        sources, targets = refs[:width], refs[width:2 * width]
        send_sem, recv_sem = refs[2 * width:]
        me = lax.axis_index(axis)
        barrier = pltpu.get_barrier_semaphore()
        for step in range(1, count):
            peer = lax.rem(me + step, count)
            pl.semaphore_signal(barrier, 1, device_id={axis: peer},
                                device_id_type=pl.DeviceIdType.MESH)
        pl.semaphore_wait(barrier, count - 1)
        copies = []
        for step in range(1, count):
            peer = lax.rem(me + step, count)
            for index in range(width):
                source = sources[index].at[peer] if splits[index] else sources[index]
                copy = pltpu.make_async_remote_copy(
                    src_ref=source, dst_ref=targets[index].at[me],
                    send_sem=send_sem.at[index, step], recv_sem=recv_sem.at[index, step],
                    device_id={axis: peer}, device_id_type=pl.DeviceIdType.MESH)
                copy.start()
                copies.append(copy)
        for index in range(width):
            if splits[index]:
                targets[index][me] = sources[index][me]
            else:
                targets[index][me] = sources[index][...]
        for copy in copies:
            copy.wait_send()
            copy.wait_recv()

    return pl.pallas_call(
        kernel,
        out_shape=[
            jax.ShapeDtypeStruct(array.shape if split else (count,) + array.shape, array.dtype)
            for array, split in parts
        ],
        in_specs=[pl.BlockSpec(memory_space=pltpu.VMEM)] * width,
        out_specs=[pl.BlockSpec(memory_space=pltpu.VMEM)] * width,
        scratch_shapes=[
            pltpu.SemaphoreType.DMA((width, count)),
            pltpu.SemaphoreType.DMA((width, count)),
        ],
        compiler_params=pltpu.CompilerParams(collective_id=tag, has_side_effects=True),
    )(*arrays)


def axis_gather(block, axis, count, tag):
    return axis_share([(block, False)], axis, count, tag)[0]


def body(
    skip_stream_arriving,
    chosen_specialists,
    sequence_piece_tallies,
    premix_rmsnorm_gain,
    dispatcher_weights,
    specialist_switch_weights,
    specialist_expand_weights,
    specialist_contract_weights,
    terminal_rmsnorm_gain,
    lexicon_projector_weights,
    softness_per_sequence,
):
    tok_rows = skip_stream_arriving.shape[0]
    experts = specialist_switch_weights.shape[0]
    columns_count = lax.axis_size("mp")
    groups = lax.axis_size("dp")
    local_squares = jnp.sum(skip_stream_arriving * skip_stream_arriving, axis=1)
    squares = jnp.sum(axis_gather(local_squares[None], "mp", columns_count, 0), axis=(0, 1))
    normed_local = (
        skip_stream_arriving
        * lax.rsqrt(squares / EMBED_DIMENSION + epsilon)[:, None]
        * premix_rmsnorm_gain
    ).astype(jnp.bfloat16)
    features_t = axis_gather(normed_local.T, "mp", columns_count, 5).reshape(
        EMBED_DIMENSION, tok_rows
    )
    by_rows = (((0,), (0,)), ((), ()))
    router = lax.dot_general(
        features_t, dispatcher_weights, by_rows, preferred_element_type=jnp.float32
    )
    mixing = jax.nn.softmax(jnp.take_along_axis(router, chosen_specialists, axis=1), axis=1)
    all_weights = lax.all_gather(
        jnp.stack(
            [
                specialist_switch_weights,
                specialist_expand_weights,
                jnp.swapaxes(specialist_contract_weights, 1, 2),
            ],
            axis=1,
        ),
        "dp", axis=2, tiled=True,
    )
    combined_t = jnp.zeros((EMBED_DIMENSION, tok_rows), jnp.float32)
    for expert in range(experts):
        weight = jnp.where(chosen_specialists[:, 0] == expert, mixing[:, 0], 0.0) + jnp.where(
            chosen_specialists[:, 1] == expert, mixing[:, 1], 0.0
        )
        gate_t = lax.dot_general(
            all_weights[expert, 0], features_t, by_rows, preferred_element_type=jnp.float32
        )
        up_t = lax.dot_general(
            all_weights[expert, 1], features_t, by_rows, preferred_element_type=jnp.float32
        )
        act_t = (jax.nn.silu(gate_t) * up_t).astype(jnp.bfloat16)
        down_t = jnp.dot(all_weights[expert, 2], act_t, preferred_element_type=jnp.float32)
        combined_t = combined_t + down_t * weight[None, :]
    ends_index = jnp.cumsum(sequence_piece_tallies[0], dtype=jnp.int32) - 1
    partial_t = combined_t.astype(jnp.bfloat16)
    column_blocks = partial_t.reshape(columns_count, -1, tok_rows)
    skip_ends = (
        axis_gather(skip_stream_arriving[ends_index], "mp", columns_count, 6)
        .transpose(1, 0, 2)
        .reshape(ends_index.shape[0], EMBED_DIMENSION)
    )
    swapped, end_partials = axis_share(
        [(column_blocks, True), (partial_t[:, ends_index].T, False)], "mp", columns_count, 7
    )
    branch = jnp.sum(swapped.astype(jnp.float32), axis=0).T
    new_hidden = skip_stream_arriving + branch_scale * branch
    end_rows = skip_ends + branch_scale * jnp.sum(end_partials.astype(jnp.float32), axis=0)
    end_squares = jnp.sum(end_rows * end_rows, axis=1)
    end_normed = (
        end_rows * lax.rsqrt(end_squares / EMBED_DIMENSION + epsilon)[:, None] * terminal_rmsnorm_gain
    ).astype(jnp.bfloat16)
    lexicon_projector_feed = axis_gather(end_normed, "dp", groups, 2).reshape(
        groups * end_normed.shape[0], EMBED_DIMENSION
    )
    lexicon_logit_values = jnp.dot(
        lexicon_projector_feed, lexicon_projector_weights, preferred_element_type=jnp.float32
    ) / (EMBED_DIMENSION / 256.0 * softness_per_sequence[:, None])
    local_max = jnp.max(lexicon_logit_values, axis=1)
    local_sum = jnp.sum(jnp.exp(lexicon_logit_values - local_max[:, None]), axis=1)
    stats = jnp.stack([local_max, local_sum])
    for axis, count, tag in (("mp", columns_count, 3), ("dp", groups, 4)):
        held = axis_gather(stats, axis, count, tag)
        top = jnp.max(held[:, 0], axis=0)
        stats = jnp.stack([top, jnp.sum(held[:, 1] * jnp.exp(held[:, 0] - top[None]), axis=0)])
    largest, total_exp = stats[0], stats[1]
    logprobs = lexicon_logit_values - largest[:, None] - jnp.log(total_exp)[:, None]
    return (new_hidden, logprobs)


def solution(mesh):
    return jax.shard_map(
        body,
        mesh=mesh,
        in_specs=(
            P("dp", "mp"),
            P("dp", None),
            P("dp", None),
            P("mp"),
            P(),
            P(None, "dp", "mp"),
            P(None, "dp", "mp"),
            P(None, "mp", "dp"),
            P(),
            P(None, ("dp", "mp")),
            P(),
        ),
        out_specs=(P("dp", "mp"), P(None, ("dp", "mp"))),
        check_vma=False,
    )
```

```python
import math

import jax
import jax.numpy as jnp
from jax import lax
from jax.experimental import pallas as pl
from jax.experimental.pallas import tpu as pltpu
from jax.sharding import PartitionSpec as P

EMBED_DIMENSION = 2304


branch_scale = 1.4 / math.sqrt(40.0)
epsilon = 1e-05


def mesh_share(parts, counts, tag):
    arrays = [array for array, _, _ in parts]
    width = len(arrays)
    axes = sorted({axis for _, axis, _ in parts})

    def kernel(*refs):
        sources, targets = refs[:width], refs[width:2 * width]
        send_sem, recv_sem = refs[2 * width:]
        barrier = pltpu.get_barrier_semaphore()
        for axis in axes:
            me = lax.axis_index(axis)
            for step in range(1, counts[axis]):
                peer = lax.rem(me + step, counts[axis])
                pl.semaphore_signal(barrier, 1, device_id={axis: peer},
                                    device_id_type=pl.DeviceIdType.MESH)
        pl.semaphore_wait(barrier, sum(counts[axis] - 1 for axis in axes))
        copies = []
        for index, (_, axis, split) in enumerate(parts):
            me = lax.axis_index(axis)
            for step in range(1, counts[axis]):
                peer = lax.rem(me + step, counts[axis])
                source = sources[index].at[peer] if split else sources[index]
                copy = pltpu.make_async_remote_copy(
                    src_ref=source, dst_ref=targets[index].at[me],
                    send_sem=send_sem.at[index, step], recv_sem=recv_sem.at[index, step],
                    device_id={axis: peer}, device_id_type=pl.DeviceIdType.MESH)
                copy.start()
                copies.append(copy)
        for index, (_, axis, split) in enumerate(parts):
            me = lax.axis_index(axis)
            if split:
                targets[index][me] = sources[index][me]
            else:
                targets[index][me] = sources[index][...]
        for copy in copies:
            copy.wait_send()
            copy.wait_recv()

    return pl.pallas_call(
        kernel,
        out_shape=[
            jax.ShapeDtypeStruct(
                array.shape if split else (counts[axis],) + array.shape, array.dtype
            )
            for array, axis, split in parts
        ],
        in_specs=[pl.BlockSpec(memory_space=pltpu.VMEM)] * width,
        out_specs=[pl.BlockSpec(memory_space=pltpu.VMEM)] * width,
        scratch_shapes=[
            pltpu.SemaphoreType.DMA((width, max(counts.values()))),
            pltpu.SemaphoreType.DMA((width, max(counts.values()))),
        ],
        compiler_params=pltpu.CompilerParams(collective_id=tag, has_side_effects=True),
    )(*arrays)


def axis_gather(block, axis, count, tag):
    return mesh_share([(block, axis, False)], {axis: count}, tag)[0]


def body(
    skip_stream_arriving,
    chosen_specialists,
    sequence_piece_tallies,
    premix_rmsnorm_gain,
    dispatcher_weights,
    specialist_switch_weights,
    specialist_expand_weights,
    specialist_contract_weights,
    terminal_rmsnorm_gain,
    lexicon_projector_weights,
    softness_per_sequence,
):
    tok_rows = skip_stream_arriving.shape[0]
    experts = specialist_switch_weights.shape[0]
    columns_count = lax.axis_size("mp")
    groups = lax.axis_size("dp")
    local_squares = jnp.sum(skip_stream_arriving * skip_stream_arriving, axis=1)
    squares = jnp.sum(axis_gather(local_squares[None], "mp", columns_count, 0), axis=(0, 1))
    normed_local = (
        skip_stream_arriving
        * lax.rsqrt(squares / EMBED_DIMENSION + epsilon)[:, None]
        * premix_rmsnorm_gain
    ).astype(jnp.bfloat16)
    features_t = axis_gather(normed_local.T, "mp", columns_count, 5).reshape(
        EMBED_DIMENSION, tok_rows
    )
    by_rows = (((0,), (0,)), ((), ()))
    router = lax.dot_general(
        features_t, dispatcher_weights, by_rows, preferred_element_type=jnp.float32
    )
    mixing = jax.nn.softmax(jnp.take_along_axis(router, chosen_specialists, axis=1), axis=1)
    all_weights = lax.all_gather(
        jnp.stack(
            [
                specialist_switch_weights,
                specialist_expand_weights,
                jnp.swapaxes(specialist_contract_weights, 1, 2),
            ],
            axis=1,
        ),
        "dp", axis=2, tiled=True,
    )
    combined_t = jnp.zeros((EMBED_DIMENSION, tok_rows), jnp.float32)
    for expert in range(experts):
        weight = jnp.where(chosen_specialists[:, 0] == expert, mixing[:, 0], 0.0) + jnp.where(
            chosen_specialists[:, 1] == expert, mixing[:, 1], 0.0
        )
        gate_t = lax.dot_general(
            all_weights[expert, 0], features_t, by_rows, preferred_element_type=jnp.float32
        )
        up_t = lax.dot_general(
            all_weights[expert, 1], features_t, by_rows, preferred_element_type=jnp.float32
        )
        act_t = (jax.nn.silu(gate_t) * up_t).astype(jnp.bfloat16)
        down_t = jnp.dot(all_weights[expert, 2], act_t, preferred_element_type=jnp.float32)
        combined_t = combined_t + down_t * weight[None, :]
    ends_index = jnp.cumsum(sequence_piece_tallies[0], dtype=jnp.int32) - 1
    partial_t = combined_t.astype(jnp.bfloat16)
    column_blocks = partial_t.reshape(columns_count, -1, tok_rows)
    end_partials, skip_ends = mesh_share(
        [
            (partial_t[:, ends_index].T, "mp", False),
            (skip_stream_arriving[ends_index], "mp", False),
        ],
        {"mp": columns_count},
        6,
    )
    skip_ends = skip_ends.transpose(1, 0, 2).reshape(ends_index.shape[0], EMBED_DIMENSION)
    end_rows = skip_ends + branch_scale * jnp.sum(end_partials.astype(jnp.float32), axis=0)
    end_squares = jnp.sum(end_rows * end_rows, axis=1)
    end_normed = (
        end_rows * lax.rsqrt(end_squares / EMBED_DIMENSION + epsilon)[:, None] * terminal_rmsnorm_gain
    ).astype(jnp.bfloat16)
    swapped, head_rows = mesh_share(
        [(column_blocks, "mp", True), (end_normed, "dp", False)],
        {"mp": columns_count, "dp": groups},
        7,
    )
    branch = jnp.sum(swapped.astype(jnp.float32), axis=0).T
    new_hidden = skip_stream_arriving + branch_scale * branch
    lexicon_projector_feed = head_rows.reshape(groups * end_normed.shape[0], EMBED_DIMENSION)
    lexicon_logit_values = jnp.dot(
        lexicon_projector_feed, lexicon_projector_weights, preferred_element_type=jnp.float32
    ) / (EMBED_DIMENSION / 256.0 * softness_per_sequence[:, None])
    local_max = jnp.max(lexicon_logit_values, axis=1)
    local_sum = jnp.sum(jnp.exp(lexicon_logit_values - local_max[:, None]), axis=1)
    stats = jnp.stack([local_max, local_sum])
    for axis, count, tag in (("mp", columns_count, 3), ("dp", groups, 4)):
        held = axis_gather(stats, axis, count, tag)
        top = jnp.max(held[:, 0], axis=0)
        stats = jnp.stack([top, jnp.sum(held[:, 1] * jnp.exp(held[:, 0] - top[None]), axis=0)])
    largest, total_exp = stats[0], stats[1]
    logprobs = lexicon_logit_values - largest[:, None] - jnp.log(total_exp)[:, None]
    return (new_hidden, logprobs)


def solution(mesh):
    return jax.shard_map(
        body,
        mesh=mesh,
        in_specs=(
            P("dp", "mp"),
            P("dp", None),
            P("dp", None),
            P("mp"),
            P(),
            P(None, "dp", "mp"),
            P(None, "dp", "mp"),
            P(None, "mp", "dp"),
            P(),
            P(None, ("dp", "mp")),
            P(),
        ),
        out_specs=(P("dp", "mp"), P(None, ("dp", "mp"))),
        check_vma=False,
    )
```

```python
import math

import jax
import jax.numpy as jnp
from jax import lax
from jax.experimental import pallas as pl
from jax.experimental.pallas import tpu as pltpu
from jax.sharding import PartitionSpec as P

EMBED_DIMENSION = 2304


branch_scale = 1.4 / math.sqrt(40.0)
epsilon = 1e-05


def mesh_share(parts, counts, tag):
    arrays = [array for array, _, _ in parts]
    width = len(arrays)
    axes = sorted({axis for _, axis, _ in parts})

    def kernel(*refs):
        sources, targets = refs[:width], refs[width:2 * width]
        send_sem, recv_sem = refs[2 * width:]
        barrier = pltpu.get_barrier_semaphore()
        for axis in axes:
            me = lax.axis_index(axis)
            for step in range(1, counts[axis]):
                peer = lax.rem(me + step, counts[axis])
                pl.semaphore_signal(barrier, 1, device_id={axis: peer},
                                    device_id_type=pl.DeviceIdType.MESH)
        pl.semaphore_wait(barrier, sum(counts[axis] - 1 for axis in axes))
        copies = []
        for index, (_, axis, split) in enumerate(parts):
            me = lax.axis_index(axis)
            for step in range(1, counts[axis]):
                peer = lax.rem(me + step, counts[axis])
                source = sources[index].at[peer] if split else sources[index]
                copy = pltpu.make_async_remote_copy(
                    src_ref=source, dst_ref=targets[index].at[me],
                    send_sem=send_sem.at[index, step], recv_sem=recv_sem.at[index, step],
                    device_id={axis: peer}, device_id_type=pl.DeviceIdType.MESH)
                copy.start()
                copies.append(copy)
        for index, (_, axis, split) in enumerate(parts):
            me = lax.axis_index(axis)
            if split:
                targets[index][me] = sources[index][me]
            else:
                targets[index][me] = sources[index][...]
        for copy in copies:
            copy.wait_send()
            copy.wait_recv()

    return pl.pallas_call(
        kernel,
        out_shape=[
            jax.ShapeDtypeStruct(
                array.shape if split else (counts[axis],) + array.shape, array.dtype
            )
            for array, axis, split in parts
        ],
        in_specs=[pl.BlockSpec(memory_space=pltpu.VMEM)] * width,
        out_specs=[pl.BlockSpec(memory_space=pltpu.VMEM)] * width,
        scratch_shapes=[
            pltpu.SemaphoreType.DMA((width, max(counts.values()))),
            pltpu.SemaphoreType.DMA((width, max(counts.values()))),
        ],
        compiler_params=pltpu.CompilerParams(collective_id=tag, has_side_effects=True),
    )(*arrays)


def axis_gather(block, axis, count, tag):
    return mesh_share([(block, axis, False)], {axis: count}, tag)[0]


def body(
    skip_stream_arriving,
    chosen_specialists,
    sequence_piece_tallies,
    premix_rmsnorm_gain,
    dispatcher_weights,
    specialist_switch_weights,
    specialist_expand_weights,
    specialist_contract_weights,
    terminal_rmsnorm_gain,
    lexicon_projector_weights,
    softness_per_sequence,
):
    tok_rows = skip_stream_arriving.shape[0]
    experts = specialist_switch_weights.shape[0]
    columns_count = lax.axis_size("mp")
    groups = lax.axis_size("dp")
    local_squares = jnp.sum(skip_stream_arriving * skip_stream_arriving, axis=1)
    squares = jnp.sum(axis_gather(local_squares[None], "mp", columns_count, 0), axis=(0, 1))
    normed_local = (
        skip_stream_arriving
        * lax.rsqrt(squares / EMBED_DIMENSION + epsilon)[:, None]
        * premix_rmsnorm_gain
    ).astype(jnp.bfloat16)
    features_t = axis_gather(normed_local.T, "mp", columns_count, 5).reshape(
        EMBED_DIMENSION, tok_rows
    )
    by_rows = (((0,), (0,)), ((), ()))
    router = lax.dot_general(
        features_t, dispatcher_weights, by_rows, preferred_element_type=jnp.float32
    )
    mixing = jax.nn.softmax(jnp.take_along_axis(router, chosen_specialists, axis=1), axis=1)
    all_weights = lax.all_gather(
        jnp.stack(
            [
                specialist_switch_weights,
                specialist_expand_weights,
                jnp.swapaxes(specialist_contract_weights, 1, 2),
            ],
            axis=1,
        ),
        "dp", axis=2, tiled=True,
    )
    combined_t = jnp.zeros((EMBED_DIMENSION, tok_rows), jnp.float32)
    for expert in range(experts):
        weight = jnp.where(chosen_specialists[:, 0] == expert, mixing[:, 0], 0.0) + jnp.where(
            chosen_specialists[:, 1] == expert, mixing[:, 1], 0.0
        )
        gate_t = lax.dot_general(
            all_weights[expert, 0], features_t, by_rows, preferred_element_type=jnp.float32
        )
        up_t = lax.dot_general(
            all_weights[expert, 1], features_t, by_rows, preferred_element_type=jnp.float32
        )
        act_t = (jax.nn.silu(gate_t) * up_t).astype(jnp.bfloat16)
        down_t = jnp.dot(all_weights[expert, 2], act_t, preferred_element_type=jnp.float32)
        combined_t = combined_t + down_t * weight[None, :]
    ends_index = jnp.cumsum(sequence_piece_tallies[0], dtype=jnp.int32) - 1
    partial_t = combined_t.astype(jnp.bfloat16)
    column_blocks = partial_t.reshape(columns_count, -1, tok_rows)
    end_partials, skip_ends = mesh_share(
        [
            (partial_t[:, ends_index].T, "mp", False),
            (skip_stream_arriving[ends_index], "mp", False),
        ],
        {"mp": columns_count},
        6,
    )
    skip_ends = skip_ends.transpose(1, 0, 2).reshape(ends_index.shape[0], EMBED_DIMENSION)
    end_rows = skip_ends + branch_scale * jnp.sum(end_partials.astype(jnp.float32), axis=0)
    end_squares = jnp.sum(end_rows * end_rows, axis=1)
    end_normed = (
        end_rows * lax.rsqrt(end_squares / EMBED_DIMENSION + epsilon)[:, None] * terminal_rmsnorm_gain
    ).astype(jnp.bfloat16)
    head_rows = axis_gather(end_normed, "dp", groups, 7)
    me = lax.axis_index("mp")
    own = lax.dynamic_index_in_dim(column_blocks, me, 0, keepdims=False)
    branch_t = own.astype(jnp.float32)
    for shift in range(1, columns_count):
        outgoing = lax.dynamic_index_in_dim(
            column_blocks, lax.rem(me + shift, columns_count), 0, keepdims=False
        )
        incoming = lax.ppermute(
            outgoing, "mp", [(i, (i + shift) % columns_count) for i in range(columns_count)]
        )
        branch_t = branch_t + incoming.astype(jnp.float32)
    branch = branch_t.T
    new_hidden = skip_stream_arriving + branch_scale * branch
    lexicon_projector_feed = head_rows.reshape(groups * end_normed.shape[0], EMBED_DIMENSION)
    lexicon_logit_values = jnp.dot(
        lexicon_projector_feed, lexicon_projector_weights, preferred_element_type=jnp.float32
    ) / (EMBED_DIMENSION / 256.0 * softness_per_sequence[:, None])
    local_max = jnp.max(lexicon_logit_values, axis=1)
    local_sum = jnp.sum(jnp.exp(lexicon_logit_values - local_max[:, None]), axis=1)
    stats = jnp.stack([local_max, local_sum])
    for axis, count, tag in (("mp", columns_count, 3), ("dp", groups, 4)):
        held = axis_gather(stats, axis, count, tag)
        top = jnp.max(held[:, 0], axis=0)
        stats = jnp.stack([top, jnp.sum(held[:, 1] * jnp.exp(held[:, 0] - top[None]), axis=0)])
    largest, total_exp = stats[0], stats[1]
    logprobs = lexicon_logit_values - largest[:, None] - jnp.log(total_exp)[:, None]
    return (new_hidden, logprobs)


def solution(mesh):
    return jax.shard_map(
        body,
        mesh=mesh,
        in_specs=(
            P("dp", "mp"),
            P("dp", None),
            P("dp", None),
            P("mp"),
            P(),
            P(None, "dp", "mp"),
            P(None, "dp", "mp"),
            P(None, "mp", "dp"),
            P(),
            P(None, ("dp", "mp")),
            P(),
        ),
        out_specs=(P("dp", "mp"), P(None, ("dp", "mp"))),
        check_vma=False,
    )
```

```python
import math

import jax
import jax.numpy as jnp
from jax import lax
from jax.experimental import pallas as pl
from jax.experimental.pallas import tpu as pltpu
from jax.sharding import PartitionSpec as P

EMBED_DIMENSION = 2304


branch_scale = 1.4 / math.sqrt(40.0)
epsilon = 1e-05


def axis_share(parts, axis, count, tag):
    arrays = [array for array, _ in parts]
    splits = [split for _, split in parts]
    width = len(arrays)

    def kernel(*refs):
        sources, targets = refs[:width], refs[width:2 * width]
        send_sem, recv_sem = refs[2 * width:]
        me = lax.axis_index(axis)
        barrier = pltpu.get_barrier_semaphore()
        for step in range(1, count):
            peer = lax.rem(me + step, count)
            pl.semaphore_signal(barrier, 1, device_id={axis: peer},
                                device_id_type=pl.DeviceIdType.MESH)
        pl.semaphore_wait(barrier, count - 1)
        copies = []
        for step in range(1, count):
            peer = lax.rem(me + step, count)
            for index in range(width):
                source = sources[index].at[peer] if splits[index] else sources[index]
                copy = pltpu.make_async_remote_copy(
                    src_ref=source, dst_ref=targets[index].at[me],
                    send_sem=send_sem.at[index, step], recv_sem=recv_sem.at[index, step],
                    device_id={axis: peer}, device_id_type=pl.DeviceIdType.MESH)
                copy.start()
                copies.append(copy)
        for index in range(width):
            if splits[index]:
                targets[index][me] = sources[index][me]
            else:
                targets[index][me] = sources[index][...]
        for copy in copies:
            copy.wait_send()
            copy.wait_recv()

    return pl.pallas_call(
        kernel,
        out_shape=[
            jax.ShapeDtypeStruct(array.shape if split else (count,) + array.shape, array.dtype)
            for array, split in parts
        ],
        in_specs=[pl.BlockSpec(memory_space=pltpu.VMEM)] * width,
        out_specs=[pl.BlockSpec(memory_space=pltpu.VMEM)] * width,
        scratch_shapes=[
            pltpu.SemaphoreType.DMA((width, count)),
            pltpu.SemaphoreType.DMA((width, count)),
        ],
        compiler_params=pltpu.CompilerParams(collective_id=tag, has_side_effects=True),
    )(*arrays)


def axis_gather(block, axis, count, tag):
    return axis_share([(block, False)], axis, count, tag)[0]


def stats_combine(tile, counts, tag):
    axes = ("mp", "dp")

    def merge(buffer):
        top = jnp.max(buffer[:, 0, :], axis=0, keepdims=True)
        total = jnp.sum(buffer[:, 1, :] * jnp.exp(buffer[:, 0, :] - top), axis=0, keepdims=True)
        return top, total

    def kernel(x_ref, out_ref, first, second, middle, send_sem, recv_sem):
        barrier = pltpu.get_barrier_semaphore()
        for axis in axes:
            me = lax.axis_index(axis)
            for step in range(1, counts[axis]):
                peer = lax.rem(me + step, counts[axis])
                pl.semaphore_signal(barrier, 1, device_id={axis: peer},
                                    device_id_type=pl.DeviceIdType.MESH)
        pl.semaphore_wait(barrier, sum(counts[axis] - 1 for axis in axes))
        stages = ((x_ref, first), (middle, second))
        for index, axis in enumerate(axes):
            source, target = stages[index]
            me = lax.axis_index(axis)
            copies = []
            for step in range(1, counts[axis]):
                peer = lax.rem(me + step, counts[axis])
                copy = pltpu.make_async_remote_copy(
                    src_ref=source, dst_ref=target.at[me],
                    send_sem=send_sem.at[index, step], recv_sem=recv_sem.at[index, step],
                    device_id={axis: peer}, device_id_type=pl.DeviceIdType.MESH)
                copy.start()
                copies.append(copy)
            target[me] = source[...]
            for copy in copies:
                copy.wait_send()
                copy.wait_recv()
            top, total = merge(target[...])
            result = out_ref if index == 1 else middle
            result[...] = jnp.zeros(result.shape, result.dtype)
            result[0:1, :] = top
            result[1:2, :] = total

    count = max(counts.values())
    return pl.pallas_call(
        kernel,
        out_shape=jax.ShapeDtypeStruct(tile.shape, tile.dtype),
        in_specs=[pl.BlockSpec(memory_space=pltpu.VMEM)],
        out_specs=pl.BlockSpec(memory_space=pltpu.VMEM),
        scratch_shapes=[
            pltpu.VMEM((counts["mp"],) + tile.shape, tile.dtype),
            pltpu.VMEM((counts["dp"],) + tile.shape, tile.dtype),
            pltpu.VMEM(tile.shape, tile.dtype),
            pltpu.SemaphoreType.DMA((2, count)),
            pltpu.SemaphoreType.DMA((2, count)),
        ],
        compiler_params=pltpu.CompilerParams(collective_id=tag, has_side_effects=True),
    )(tile)


def body(
    skip_stream_arriving,
    chosen_specialists,
    sequence_piece_tallies,
    premix_rmsnorm_gain,
    dispatcher_weights,
    specialist_switch_weights,
    specialist_expand_weights,
    specialist_contract_weights,
    terminal_rmsnorm_gain,
    lexicon_projector_weights,
    softness_per_sequence,
):
    tok_rows = skip_stream_arriving.shape[0]
    experts = specialist_switch_weights.shape[0]
    columns_count = lax.axis_size("mp")
    groups = lax.axis_size("dp")
    local_squares = jnp.sum(skip_stream_arriving * skip_stream_arriving, axis=1)
    squares = jnp.sum(axis_gather(local_squares[None], "mp", columns_count, 0), axis=(0, 1))
    normed_local = (
        skip_stream_arriving
        * lax.rsqrt(squares / EMBED_DIMENSION + epsilon)[:, None]
        * premix_rmsnorm_gain
    ).astype(jnp.bfloat16)
    features_t = axis_gather(normed_local.T, "mp", columns_count, 5).reshape(
        EMBED_DIMENSION, tok_rows
    )
    by_rows = (((0,), (0,)), ((), ()))
    router = lax.dot_general(
        features_t, dispatcher_weights, by_rows, preferred_element_type=jnp.float32
    )
    mixing = jax.nn.softmax(jnp.take_along_axis(router, chosen_specialists, axis=1), axis=1)
    all_weights = lax.all_gather(
        jnp.stack(
            [
                specialist_switch_weights,
                specialist_expand_weights,
                jnp.swapaxes(specialist_contract_weights, 1, 2),
            ],
            axis=1,
        ),
        "dp", axis=2, tiled=True,
    )
    combined_t = jnp.zeros((EMBED_DIMENSION, tok_rows), jnp.float32)
    for expert in range(experts):
        weight = jnp.where(chosen_specialists[:, 0] == expert, mixing[:, 0], 0.0) + jnp.where(
            chosen_specialists[:, 1] == expert, mixing[:, 1], 0.0
        )
        gate_t = lax.dot_general(
            all_weights[expert, 0], features_t, by_rows, preferred_element_type=jnp.float32
        )
        up_t = lax.dot_general(
            all_weights[expert, 1], features_t, by_rows, preferred_element_type=jnp.float32
        )
        act_t = (jax.nn.silu(gate_t) * up_t).astype(jnp.bfloat16)
        down_t = jnp.dot(all_weights[expert, 2], act_t, preferred_element_type=jnp.float32)
        combined_t = combined_t + down_t * weight[None, :]
    ends_index = jnp.cumsum(sequence_piece_tallies[0], dtype=jnp.int32) - 1
    partial_t = combined_t.astype(jnp.bfloat16)
    column_blocks = partial_t.reshape(columns_count, -1, tok_rows)
    skip_ends = (
        axis_gather(skip_stream_arriving[ends_index], "mp", columns_count, 6)
        .transpose(1, 0, 2)
        .reshape(ends_index.shape[0], EMBED_DIMENSION)
    )
    swapped, end_partials = axis_share(
        [(column_blocks, True), (partial_t[:, ends_index].T, False)], "mp", columns_count, 7
    )
    branch = jnp.sum(swapped.astype(jnp.float32), axis=0).T
    new_hidden = skip_stream_arriving + branch_scale * branch
    end_rows = skip_ends + branch_scale * jnp.sum(end_partials.astype(jnp.float32), axis=0)
    end_squares = jnp.sum(end_rows * end_rows, axis=1)
    end_normed = (
        end_rows * lax.rsqrt(end_squares / EMBED_DIMENSION + epsilon)[:, None] * terminal_rmsnorm_gain
    ).astype(jnp.bfloat16)
    lexicon_projector_feed = axis_gather(end_normed, "dp", groups, 2).reshape(
        groups * end_normed.shape[0], EMBED_DIMENSION
    )
    lexicon_logit_values = jnp.dot(
        lexicon_projector_feed, lexicon_projector_weights, preferred_element_type=jnp.float32
    ) / (EMBED_DIMENSION / 256.0 * softness_per_sequence[:, None])
    local_max = jnp.max(lexicon_logit_values, axis=1)
    local_sum = jnp.sum(jnp.exp(lexicon_logit_values - local_max[:, None]), axis=1)
    requests = local_max.shape[0]
    tile = jnp.zeros((8, 128), jnp.float32)
    tile = tile.at[0, :requests].set(local_max).at[1, :requests].set(local_sum)
    merged = stats_combine(tile, {"mp": columns_count, "dp": groups}, 3)
    largest, total_exp = merged[0, :requests], merged[1, :requests]
    logprobs = lexicon_logit_values - largest[:, None] - jnp.log(total_exp)[:, None]
    return (new_hidden, logprobs)


def solution(mesh):
    return jax.shard_map(
        body,
        mesh=mesh,
        in_specs=(
            P("dp", "mp"),
            P("dp", None),
            P("dp", None),
            P("mp"),
            P(),
            P(None, "dp", "mp"),
            P(None, "dp", "mp"),
            P(None, "mp", "dp"),
            P(),
            P(None, ("dp", "mp")),
            P(),
        ),
        out_specs=(P("dp", "mp"), P(None, ("dp", "mp"))),
        check_vma=False,
    )
```

```python
import math

import jax
import jax.numpy as jnp
from jax import lax
from jax.experimental import pallas as pl
from jax.experimental.pallas import tpu as pltpu
from jax.sharding import PartitionSpec as P

EMBED_DIMENSION = 2304


branch_scale = 1.4 / math.sqrt(40.0)
epsilon = 1e-05


def axis_share(parts, axis, count, tag):
    arrays = [array for array, _ in parts]
    splits = [split for _, split in parts]
    width = len(arrays)

    def kernel(*refs):
        sources, targets = refs[:width], refs[width:2 * width]
        send_sem, recv_sem = refs[2 * width:]
        me = lax.axis_index(axis)
        barrier = pltpu.get_barrier_semaphore()
        for step in range(1, count):
            peer = lax.rem(me + step, count)
            pl.semaphore_signal(barrier, 1, device_id={axis: peer},
                                device_id_type=pl.DeviceIdType.MESH)
        pl.semaphore_wait(barrier, count - 1)
        copies = []
        for step in range(1, count):
            peer = lax.rem(me + step, count)
            for index in range(width):
                source = sources[index].at[peer] if splits[index] else sources[index]
                copy = pltpu.make_async_remote_copy(
                    src_ref=source, dst_ref=targets[index].at[me],
                    send_sem=send_sem.at[index, step], recv_sem=recv_sem.at[index, step],
                    device_id={axis: peer}, device_id_type=pl.DeviceIdType.MESH)
                copy.start()
                copies.append(copy)
        for index in range(width):
            if splits[index]:
                targets[index][me] = sources[index][me]
            else:
                targets[index][me] = sources[index][...]
        for copy in copies:
            copy.wait_send()
            copy.wait_recv()

    return pl.pallas_call(
        kernel,
        out_shape=[
            jax.ShapeDtypeStruct(array.shape if split else (count,) + array.shape, array.dtype)
            for array, split in parts
        ],
        in_specs=[pl.BlockSpec(memory_space=pltpu.VMEM)] * width,
        out_specs=[pl.BlockSpec(memory_space=pltpu.VMEM)] * width,
        scratch_shapes=[
            pltpu.SemaphoreType.DMA((width, count)),
            pltpu.SemaphoreType.DMA((width, count)),
        ],
        compiler_params=pltpu.CompilerParams(collective_id=tag, has_side_effects=True),
    )(*arrays)


def axis_gather(block, axis, count, tag):
    return axis_share([(block, False)], axis, count, tag)[0]


def stats_combine(tile, counts, tag):
    axes = ("mp", "dp")

    def merge(buffer):
        top = jnp.max(buffer[:, 0, :], axis=0, keepdims=True)
        total = jnp.sum(buffer[:, 1, :] * jnp.exp(buffer[:, 0, :] - top), axis=0, keepdims=True)
        return top, total

    def kernel(x_ref, out_ref, first, second, middle, send_sem, recv_sem):
        barrier = pltpu.get_barrier_semaphore()
        for axis in axes:
            me = lax.axis_index(axis)
            for step in range(1, counts[axis]):
                peer = lax.rem(me + step, counts[axis])
                pl.semaphore_signal(barrier, 1, device_id={axis: peer},
                                    device_id_type=pl.DeviceIdType.MESH)
        pl.semaphore_wait(barrier, sum(counts[axis] - 1 for axis in axes))
        stages = ((x_ref, first), (middle, second))
        for index, axis in enumerate(axes):
            source, target = stages[index]
            me = lax.axis_index(axis)
            copies = []
            for step in range(1, counts[axis]):
                peer = lax.rem(me + step, counts[axis])
                copy = pltpu.make_async_remote_copy(
                    src_ref=source, dst_ref=target.at[me],
                    send_sem=send_sem.at[index, step], recv_sem=recv_sem.at[index, step],
                    device_id={axis: peer}, device_id_type=pl.DeviceIdType.MESH)
                copy.start()
                copies.append(copy)
            target[me] = source[...]
            for copy in copies:
                copy.wait_send()
                copy.wait_recv()
            top, total = merge(target[...])
            result = out_ref if index == 1 else middle
            result[...] = jnp.zeros(result.shape, result.dtype)
            result[0:1, :] = top
            result[1:2, :] = total

    count = max(counts.values())
    return pl.pallas_call(
        kernel,
        out_shape=jax.ShapeDtypeStruct(tile.shape, tile.dtype),
        in_specs=[pl.BlockSpec(memory_space=pltpu.VMEM)],
        out_specs=pl.BlockSpec(memory_space=pltpu.VMEM),
        scratch_shapes=[
            pltpu.VMEM((counts["mp"],) + tile.shape, tile.dtype),
            pltpu.VMEM((counts["dp"],) + tile.shape, tile.dtype),
            pltpu.VMEM(tile.shape, tile.dtype),
            pltpu.SemaphoreType.DMA((2, count)),
            pltpu.SemaphoreType.DMA((2, count)),
        ],
        compiler_params=pltpu.CompilerParams(collective_id=tag, has_side_effects=True),
    )(tile)


def tail_exchange(blocks, end_parts, skip_ends, gain, counts, tag):
    rows = end_parts.shape[0]

    def kernel(blocks_ref, parts_ref, skip_ref, gain_ref, swapped_ref, head_ref,
               parts_held, normed, send_sem, recv_sem):
        barrier = pltpu.get_barrier_semaphore()
        for axis in ("mp", "dp"):
            me = lax.axis_index(axis)
            for step in range(1, counts[axis]):
                peer = lax.rem(me + step, counts[axis])
                pl.semaphore_signal(barrier, 1, device_id={axis: peer},
                                    device_id_type=pl.DeviceIdType.MESH)
        pl.semaphore_wait(barrier, counts["mp"] + counts["dp"] - 2)
        me = lax.axis_index("mp")
        block_copies, part_copies = [], []
        for step in range(1, counts["mp"]):
            peer = lax.rem(me + step, counts["mp"])
            copy = pltpu.make_async_remote_copy(
                src_ref=parts_ref, dst_ref=parts_held.at[me],
                send_sem=send_sem.at[0, step], recv_sem=recv_sem.at[0, step],
                device_id={"mp": peer}, device_id_type=pl.DeviceIdType.MESH)
            copy.start()
            part_copies.append(copy)
        for step in range(1, counts["mp"]):
            peer = lax.rem(me + step, counts["mp"])
            copy = pltpu.make_async_remote_copy(
                src_ref=blocks_ref.at[peer], dst_ref=swapped_ref.at[me],
                send_sem=send_sem.at[1, step], recv_sem=recv_sem.at[1, step],
                device_id={"mp": peer}, device_id_type=pl.DeviceIdType.MESH)
            copy.start()
            block_copies.append(copy)
        parts_held[me] = parts_ref[...]
        swapped_ref[me] = blocks_ref[me]
        for copy in part_copies:
            copy.wait_send()
            copy.wait_recv()
        total = jnp.sum(parts_held[...].astype(jnp.float32), axis=0)
        end_rows = skip_ref[...] + branch_scale * total
        squares = jnp.sum(end_rows * end_rows, axis=1, keepdims=True)
        normed[...] = (
            end_rows * lax.rsqrt(squares / EMBED_DIMENSION + epsilon) * gain_ref[...]
        ).astype(normed.dtype)
        group = lax.axis_index("dp")
        head_copies = []
        for step in range(1, counts["dp"]):
            peer = lax.rem(group + step, counts["dp"])
            copy = pltpu.make_async_remote_copy(
                src_ref=normed, dst_ref=head_ref.at[group],
                send_sem=send_sem.at[2, step], recv_sem=recv_sem.at[2, step],
                device_id={"dp": peer}, device_id_type=pl.DeviceIdType.MESH)
            copy.start()
            head_copies.append(copy)
        head_ref[group] = normed[...]
        for copy in block_copies + head_copies:
            copy.wait_send()
            copy.wait_recv()

    count = max(counts.values())
    return pl.pallas_call(
        kernel,
        out_shape=[
            jax.ShapeDtypeStruct(blocks.shape, blocks.dtype),
            jax.ShapeDtypeStruct((counts["dp"], rows, EMBED_DIMENSION), jnp.bfloat16),
        ],
        in_specs=[pl.BlockSpec(memory_space=pltpu.VMEM)] * 4,
        out_specs=[pl.BlockSpec(memory_space=pltpu.VMEM)] * 2,
        scratch_shapes=[
            pltpu.VMEM((counts["mp"],) + end_parts.shape, end_parts.dtype),
            pltpu.VMEM((rows, EMBED_DIMENSION), jnp.bfloat16),
            pltpu.SemaphoreType.DMA((3, count)),
            pltpu.SemaphoreType.DMA((3, count)),
        ],
        compiler_params=pltpu.CompilerParams(collective_id=tag, has_side_effects=True),
    )(blocks, end_parts, skip_ends, gain)


def body(
    skip_stream_arriving,
    chosen_specialists,
    sequence_piece_tallies,
    premix_rmsnorm_gain,
    dispatcher_weights,
    specialist_switch_weights,
    specialist_expand_weights,
    specialist_contract_weights,
    terminal_rmsnorm_gain,
    lexicon_projector_weights,
    softness_per_sequence,
):
    tok_rows = skip_stream_arriving.shape[0]
    experts = specialist_switch_weights.shape[0]
    columns_count = lax.axis_size("mp")
    groups = lax.axis_size("dp")
    local_squares = jnp.sum(skip_stream_arriving * skip_stream_arriving, axis=1)
    squares = jnp.sum(axis_gather(local_squares[None], "mp", columns_count, 0), axis=(0, 1))
    normed_local = (
        skip_stream_arriving
        * lax.rsqrt(squares / EMBED_DIMENSION + epsilon)[:, None]
        * premix_rmsnorm_gain
    ).astype(jnp.bfloat16)
    features_t = axis_gather(normed_local.T, "mp", columns_count, 5).reshape(
        EMBED_DIMENSION, tok_rows
    )
    by_rows = (((0,), (0,)), ((), ()))
    router = lax.dot_general(
        features_t, dispatcher_weights, by_rows, preferred_element_type=jnp.float32
    )
    mixing = jax.nn.softmax(jnp.take_along_axis(router, chosen_specialists, axis=1), axis=1)
    all_weights = lax.all_gather(
        jnp.stack(
            [
                specialist_switch_weights,
                specialist_expand_weights,
                jnp.swapaxes(specialist_contract_weights, 1, 2),
            ],
            axis=1,
        ),
        "dp", axis=2, tiled=True,
    )
    combined_t = jnp.zeros((EMBED_DIMENSION, tok_rows), jnp.float32)
    for expert in range(experts):
        weight = jnp.where(chosen_specialists[:, 0] == expert, mixing[:, 0], 0.0) + jnp.where(
            chosen_specialists[:, 1] == expert, mixing[:, 1], 0.0
        )
        gate_t = lax.dot_general(
            all_weights[expert, 0], features_t, by_rows, preferred_element_type=jnp.float32
        )
        up_t = lax.dot_general(
            all_weights[expert, 1], features_t, by_rows, preferred_element_type=jnp.float32
        )
        act_t = (jax.nn.silu(gate_t) * up_t).astype(jnp.bfloat16)
        down_t = jnp.dot(all_weights[expert, 2], act_t, preferred_element_type=jnp.float32)
        combined_t = combined_t + down_t * weight[None, :]
    ends_index = jnp.cumsum(sequence_piece_tallies[0], dtype=jnp.int32) - 1
    partial_t = combined_t.astype(jnp.bfloat16)
    column_blocks = partial_t.reshape(columns_count, -1, tok_rows)
    skip_ends = (
        axis_gather(skip_stream_arriving[ends_index], "mp", columns_count, 6)
        .transpose(1, 0, 2)
        .reshape(ends_index.shape[0], EMBED_DIMENSION)
    )
    swapped, head_rows = tail_exchange(
        column_blocks,
        partial_t[:, ends_index].T,
        skip_ends,
        terminal_rmsnorm_gain[None],
        {"mp": columns_count, "dp": groups},
        7,
    )
    branch = jnp.sum(swapped.astype(jnp.float32), axis=0).T
    new_hidden = skip_stream_arriving + branch_scale * branch
    lexicon_projector_feed = head_rows.reshape(groups * ends_index.shape[0], EMBED_DIMENSION)
    lexicon_logit_values = jnp.dot(
        lexicon_projector_feed, lexicon_projector_weights, preferred_element_type=jnp.float32
    ) / (EMBED_DIMENSION / 256.0 * softness_per_sequence[:, None])
    local_max = jnp.max(lexicon_logit_values, axis=1)
    local_sum = jnp.sum(jnp.exp(lexicon_logit_values - local_max[:, None]), axis=1)
    requests = local_max.shape[0]
    tile = jnp.zeros((8, 128), jnp.float32)
    tile = tile.at[0, :requests].set(local_max).at[1, :requests].set(local_sum)
    merged = stats_combine(tile, {"mp": columns_count, "dp": groups}, 3)
    largest, total_exp = merged[0, :requests], merged[1, :requests]
    logprobs = lexicon_logit_values - largest[:, None] - jnp.log(total_exp)[:, None]
    return (new_hidden, logprobs)


def solution(mesh):
    return jax.shard_map(
        body,
        mesh=mesh,
        in_specs=(
            P("dp", "mp"),
            P("dp", None),
            P("dp", None),
            P("mp"),
            P(),
            P(None, "dp", "mp"),
            P(None, "dp", "mp"),
            P(None, "mp", "dp"),
            P(),
            P(None, ("dp", "mp")),
            P(),
        ),
        out_specs=(P("dp", "mp"), P(None, ("dp", "mp"))),
        check_vma=False,
    )
```

```python
import math

import jax
import jax.numpy as jnp
from jax import lax
from jax.experimental import pallas as pl
from jax.experimental.pallas import tpu as pltpu
from jax.sharding import PartitionSpec as P

EMBED_DIMENSION = 2304


branch_scale = 1.4 / math.sqrt(40.0)
epsilon = 1e-05


def axis_share(parts, axis, count, tag):
    arrays = [array for array, _ in parts]
    splits = [split for _, split in parts]
    width = len(arrays)

    def kernel(*refs):
        sources, targets = refs[:width], refs[width:2 * width]
        send_sem, recv_sem = refs[2 * width:]
        me = lax.axis_index(axis)
        barrier = pltpu.get_barrier_semaphore()
        for step in range(1, count):
            peer = lax.rem(me + step, count)
            pl.semaphore_signal(barrier, 1, device_id={axis: peer},
                                device_id_type=pl.DeviceIdType.MESH)
        pl.semaphore_wait(barrier, count - 1)
        copies = []
        for step in range(1, count):
            peer = lax.rem(me + step, count)
            for index in range(width):
                source = sources[index].at[peer] if splits[index] else sources[index]
                copy = pltpu.make_async_remote_copy(
                    src_ref=source, dst_ref=targets[index].at[me],
                    send_sem=send_sem.at[index, step], recv_sem=recv_sem.at[index, step],
                    device_id={axis: peer}, device_id_type=pl.DeviceIdType.MESH)
                copy.start()
                copies.append(copy)
        for index in range(width):
            if splits[index]:
                targets[index][me] = sources[index][me]
            else:
                targets[index][me] = sources[index][...]
        for copy in copies:
            copy.wait_send()
            copy.wait_recv()

    return pl.pallas_call(
        kernel,
        out_shape=[
            jax.ShapeDtypeStruct(array.shape if split else (count,) + array.shape, array.dtype)
            for array, split in parts
        ],
        in_specs=[pl.BlockSpec(memory_space=pltpu.VMEM)] * width,
        out_specs=[pl.BlockSpec(memory_space=pltpu.VMEM)] * width,
        scratch_shapes=[
            pltpu.SemaphoreType.DMA((width, count)),
            pltpu.SemaphoreType.DMA((width, count)),
        ],
        compiler_params=pltpu.CompilerParams(collective_id=tag, has_side_effects=True),
    )(*arrays)


def axis_gather(block, axis, count, tag):
    return axis_share([(block, False)], axis, count, tag)[0]


def stats_combine(tile, blocks, counts, tag):
    axes = ("mp", "dp")

    def merge(buffer):
        top = jnp.max(buffer[:, 0, :], axis=0, keepdims=True)
        total = jnp.sum(buffer[:, 1, :] * jnp.exp(buffer[:, 0, :] - top), axis=0, keepdims=True)
        return top, total

    def kernel(x_ref, blocks_ref, out_ref, swapped_ref, first, second, middle, send_sem, recv_sem):
        barrier = pltpu.get_barrier_semaphore()
        for axis in axes:
            me = lax.axis_index(axis)
            for step in range(1, counts[axis]):
                peer = lax.rem(me + step, counts[axis])
                pl.semaphore_signal(barrier, 1, device_id={axis: peer},
                                    device_id_type=pl.DeviceIdType.MESH)
        pl.semaphore_wait(barrier, sum(counts[axis] - 1 for axis in axes))
        column = lax.axis_index("mp")
        block_copies = []
        for step in range(1, counts["mp"]):
            peer = lax.rem(column + step, counts["mp"])
            copy = pltpu.make_async_remote_copy(
                src_ref=blocks_ref.at[peer], dst_ref=swapped_ref.at[column],
                send_sem=send_sem.at[2, step], recv_sem=recv_sem.at[2, step],
                device_id={"mp": peer}, device_id_type=pl.DeviceIdType.MESH)
            copy.start()
            block_copies.append(copy)
        swapped_ref[column] = blocks_ref[column]
        stages = ((x_ref, first), (middle, second))
        for index, axis in enumerate(axes):
            source, target = stages[index]
            me = lax.axis_index(axis)
            copies = []
            for step in range(1, counts[axis]):
                peer = lax.rem(me + step, counts[axis])
                copy = pltpu.make_async_remote_copy(
                    src_ref=source, dst_ref=target.at[me],
                    send_sem=send_sem.at[index, step], recv_sem=recv_sem.at[index, step],
                    device_id={axis: peer}, device_id_type=pl.DeviceIdType.MESH)
                copy.start()
                copies.append(copy)
            target[me] = source[...]
            for copy in copies:
                copy.wait_send()
                copy.wait_recv()
            top, total = merge(target[...])
            result = out_ref if index == 1 else middle
            result[...] = jnp.zeros(result.shape, result.dtype)
            result[0:1, :] = top
            result[1:2, :] = total
        for copy in block_copies:
            copy.wait_send()
            copy.wait_recv()

    count = max(counts.values())
    return pl.pallas_call(
        kernel,
        out_shape=[
            jax.ShapeDtypeStruct(tile.shape, tile.dtype),
            jax.ShapeDtypeStruct(blocks.shape, blocks.dtype),
        ],
        in_specs=[pl.BlockSpec(memory_space=pltpu.VMEM)] * 2,
        out_specs=[pl.BlockSpec(memory_space=pltpu.VMEM)] * 2,
        scratch_shapes=[
            pltpu.VMEM((counts["mp"],) + tile.shape, tile.dtype),
            pltpu.VMEM((counts["dp"],) + tile.shape, tile.dtype),
            pltpu.VMEM(tile.shape, tile.dtype),
            pltpu.SemaphoreType.DMA((3, count)),
            pltpu.SemaphoreType.DMA((3, count)),
        ],
        compiler_params=pltpu.CompilerParams(collective_id=tag, has_side_effects=True),
    )(tile, blocks)


def tail_exchange(end_parts, skip_ends, gain, counts, tag):
    rows = end_parts.shape[0]

    def kernel(parts_ref, skip_ref, gain_ref, head_ref, parts_held, normed, send_sem, recv_sem):
        barrier = pltpu.get_barrier_semaphore()
        for axis in ("mp", "dp"):
            me = lax.axis_index(axis)
            for step in range(1, counts[axis]):
                peer = lax.rem(me + step, counts[axis])
                pl.semaphore_signal(barrier, 1, device_id={axis: peer},
                                    device_id_type=pl.DeviceIdType.MESH)
        pl.semaphore_wait(barrier, counts["mp"] + counts["dp"] - 2)
        me = lax.axis_index("mp")
        part_copies = []
        for step in range(1, counts["mp"]):
            peer = lax.rem(me + step, counts["mp"])
            copy = pltpu.make_async_remote_copy(
                src_ref=parts_ref, dst_ref=parts_held.at[me],
                send_sem=send_sem.at[0, step], recv_sem=recv_sem.at[0, step],
                device_id={"mp": peer}, device_id_type=pl.DeviceIdType.MESH)
            copy.start()
            part_copies.append(copy)
        parts_held[me] = parts_ref[...]
        for copy in part_copies:
            copy.wait_send()
            copy.wait_recv()
        total = jnp.sum(parts_held[...].astype(jnp.float32), axis=0)
        end_rows = skip_ref[...] + branch_scale * total
        squares = jnp.sum(end_rows * end_rows, axis=1, keepdims=True)
        normed[...] = (
            end_rows * lax.rsqrt(squares / EMBED_DIMENSION + epsilon) * gain_ref[...]
        ).astype(normed.dtype)
        group = lax.axis_index("dp")
        head_copies = []
        for step in range(1, counts["dp"]):
            peer = lax.rem(group + step, counts["dp"])
            copy = pltpu.make_async_remote_copy(
                src_ref=normed, dst_ref=head_ref.at[group],
                send_sem=send_sem.at[2, step], recv_sem=recv_sem.at[2, step],
                device_id={"dp": peer}, device_id_type=pl.DeviceIdType.MESH)
            copy.start()
            head_copies.append(copy)
        head_ref[group] = normed[...]
        for copy in head_copies:
            copy.wait_send()
            copy.wait_recv()

    count = max(counts.values())
    return pl.pallas_call(
        kernel,
        out_shape=jax.ShapeDtypeStruct((counts["dp"], rows, EMBED_DIMENSION), jnp.bfloat16),
        in_specs=[pl.BlockSpec(memory_space=pltpu.VMEM)] * 3,
        out_specs=pl.BlockSpec(memory_space=pltpu.VMEM),
        scratch_shapes=[
            pltpu.VMEM((counts["mp"],) + end_parts.shape, end_parts.dtype),
            pltpu.VMEM((rows, EMBED_DIMENSION), jnp.bfloat16),
            pltpu.SemaphoreType.DMA((3, count)),
            pltpu.SemaphoreType.DMA((3, count)),
        ],
        compiler_params=pltpu.CompilerParams(collective_id=tag, has_side_effects=True),
    )(end_parts, skip_ends, gain)


def body(
    skip_stream_arriving,
    chosen_specialists,
    sequence_piece_tallies,
    premix_rmsnorm_gain,
    dispatcher_weights,
    specialist_switch_weights,
    specialist_expand_weights,
    specialist_contract_weights,
    terminal_rmsnorm_gain,
    lexicon_projector_weights,
    softness_per_sequence,
):
    tok_rows = skip_stream_arriving.shape[0]
    experts = specialist_switch_weights.shape[0]
    columns_count = lax.axis_size("mp")
    groups = lax.axis_size("dp")
    local_squares = jnp.sum(skip_stream_arriving * skip_stream_arriving, axis=1)
    squares = jnp.sum(axis_gather(local_squares[None], "mp", columns_count, 0), axis=(0, 1))
    normed_local = (
        skip_stream_arriving
        * lax.rsqrt(squares / EMBED_DIMENSION + epsilon)[:, None]
        * premix_rmsnorm_gain
    ).astype(jnp.bfloat16)
    features_t = axis_gather(normed_local.T, "mp", columns_count, 5).reshape(
        EMBED_DIMENSION, tok_rows
    )
    by_rows = (((0,), (0,)), ((), ()))
    router = lax.dot_general(
        features_t, dispatcher_weights, by_rows, preferred_element_type=jnp.float32
    )
    mixing = jax.nn.softmax(jnp.take_along_axis(router, chosen_specialists, axis=1), axis=1)
    all_weights = lax.all_gather(
        jnp.stack(
            [
                specialist_switch_weights,
                specialist_expand_weights,
                jnp.swapaxes(specialist_contract_weights, 1, 2),
            ],
            axis=1,
        ),
        "dp", axis=2, tiled=True,
    )
    combined_t = jnp.zeros((EMBED_DIMENSION, tok_rows), jnp.float32)
    for expert in range(experts):
        weight = jnp.where(chosen_specialists[:, 0] == expert, mixing[:, 0], 0.0) + jnp.where(
            chosen_specialists[:, 1] == expert, mixing[:, 1], 0.0
        )
        gate_t = lax.dot_general(
            all_weights[expert, 0], features_t, by_rows, preferred_element_type=jnp.float32
        )
        up_t = lax.dot_general(
            all_weights[expert, 1], features_t, by_rows, preferred_element_type=jnp.float32
        )
        act_t = (jax.nn.silu(gate_t) * up_t).astype(jnp.bfloat16)
        down_t = jnp.dot(all_weights[expert, 2], act_t, preferred_element_type=jnp.float32)
        combined_t = combined_t + down_t * weight[None, :]
    ends_index = jnp.cumsum(sequence_piece_tallies[0], dtype=jnp.int32) - 1
    partial_t = combined_t.astype(jnp.bfloat16)
    column_blocks = partial_t.reshape(columns_count, -1, tok_rows)
    skip_ends = (
        axis_gather(skip_stream_arriving[ends_index], "mp", columns_count, 6)
        .transpose(1, 0, 2)
        .reshape(ends_index.shape[0], EMBED_DIMENSION)
    )
    head_rows = tail_exchange(
        partial_t[:, ends_index].T,
        skip_ends,
        terminal_rmsnorm_gain[None],
        {"mp": columns_count, "dp": groups},
        7,
    )
    lexicon_projector_feed = head_rows.reshape(groups * ends_index.shape[0], EMBED_DIMENSION)
    lexicon_logit_values = jnp.dot(
        lexicon_projector_feed, lexicon_projector_weights, preferred_element_type=jnp.float32
    ) / (EMBED_DIMENSION / 256.0 * softness_per_sequence[:, None])
    local_max = jnp.max(lexicon_logit_values, axis=1)
    local_sum = jnp.sum(jnp.exp(lexicon_logit_values - local_max[:, None]), axis=1)
    requests = local_max.shape[0]
    tile = jnp.zeros((8, 128), jnp.float32)
    tile = tile.at[0, :requests].set(local_max).at[1, :requests].set(local_sum)
    merged, swapped = stats_combine(tile, column_blocks, {"mp": columns_count, "dp": groups}, 3)
    branch = jnp.sum(swapped.astype(jnp.float32), axis=0).T
    new_hidden = skip_stream_arriving + branch_scale * branch
    largest, total_exp = merged[0, :requests], merged[1, :requests]
    logprobs = lexicon_logit_values - largest[:, None] - jnp.log(total_exp)[:, None]
    return (new_hidden, logprobs)


def solution(mesh):
    return jax.shard_map(
        body,
        mesh=mesh,
        in_specs=(
            P("dp", "mp"),
            P("dp", None),
            P("dp", None),
            P("mp"),
            P(),
            P(None, "dp", "mp"),
            P(None, "dp", "mp"),
            P(None, "mp", "dp"),
            P(),
            P(None, ("dp", "mp")),
            P(),
        ),
        out_specs=(P("dp", "mp"), P(None, ("dp", "mp"))),
        check_vma=False,
    )
```

```python
import math

import jax
import jax.numpy as jnp
from jax import lax
from jax.experimental import pallas as pl
from jax.experimental.pallas import tpu as pltpu
from jax.sharding import PartitionSpec as P

EMBED_DIMENSION = 2304


branch_scale = 1.4 / math.sqrt(40.0)
epsilon = 1e-05


def axis_share(parts, axis, count, tag):
    arrays = [array for array, _ in parts]
    splits = [split for _, split in parts]
    width = len(arrays)

    def kernel(*refs):
        sources, targets = refs[:width], refs[width:2 * width]
        send_sem, recv_sem = refs[2 * width:]
        me = lax.axis_index(axis)
        barrier = pltpu.get_barrier_semaphore()
        for step in range(1, count):
            peer = lax.rem(me + step, count)
            pl.semaphore_signal(barrier, 1, device_id={axis: peer},
                                device_id_type=pl.DeviceIdType.MESH)
        pl.semaphore_wait(barrier, count - 1)
        copies = []
        for step in range(1, count):
            peer = lax.rem(me + step, count)
            for index in range(width):
                source = sources[index].at[peer] if splits[index] else sources[index]
                copy = pltpu.make_async_remote_copy(
                    src_ref=source, dst_ref=targets[index].at[me],
                    send_sem=send_sem.at[index, step], recv_sem=recv_sem.at[index, step],
                    device_id={axis: peer}, device_id_type=pl.DeviceIdType.MESH)
                copy.start()
                copies.append(copy)
        for index in range(width):
            if splits[index]:
                targets[index][me] = sources[index][me]
            else:
                targets[index][me] = sources[index][...]
        for copy in copies:
            copy.wait_send()
            copy.wait_recv()

    return pl.pallas_call(
        kernel,
        out_shape=[
            jax.ShapeDtypeStruct(array.shape if split else (count,) + array.shape, array.dtype)
            for array, split in parts
        ],
        in_specs=[pl.BlockSpec(memory_space=pltpu.VMEM)] * width,
        out_specs=[pl.BlockSpec(memory_space=pltpu.VMEM)] * width,
        scratch_shapes=[
            pltpu.SemaphoreType.DMA((width, count)),
            pltpu.SemaphoreType.DMA((width, count)),
        ],
        compiler_params=pltpu.CompilerParams(collective_id=tag, has_side_effects=True),
    )(*arrays)


def axis_gather(block, axis, count, tag):
    return axis_share([(block, False)], axis, count, tag)[0]


def stats_combine(tile, counts, tag):
    axes = ("mp", "dp")

    def merge(buffer):
        top = jnp.max(buffer[:, 0, :], axis=0, keepdims=True)
        total = jnp.sum(buffer[:, 1, :] * jnp.exp(buffer[:, 0, :] - top), axis=0, keepdims=True)
        return top, total

    def kernel(x_ref, out_ref, first, second, middle, send_sem, recv_sem):
        barrier = pltpu.get_barrier_semaphore()
        for axis in axes:
            me = lax.axis_index(axis)
            for step in range(1, counts[axis]):
                peer = lax.rem(me + step, counts[axis])
                pl.semaphore_signal(barrier, 1, device_id={axis: peer},
                                    device_id_type=pl.DeviceIdType.MESH)
        pl.semaphore_wait(barrier, sum(counts[axis] - 1 for axis in axes))
        stages = ((x_ref, first), (middle, second))
        for index, axis in enumerate(axes):
            source, target = stages[index]
            me = lax.axis_index(axis)
            copies = []
            for step in range(1, counts[axis]):
                peer = lax.rem(me + step, counts[axis])
                copy = pltpu.make_async_remote_copy(
                    src_ref=source, dst_ref=target.at[me],
                    send_sem=send_sem.at[index, step], recv_sem=recv_sem.at[index, step],
                    device_id={axis: peer}, device_id_type=pl.DeviceIdType.MESH)
                copy.start()
                copies.append(copy)
            target[me] = source[...]
            for copy in copies:
                copy.wait_send()
                copy.wait_recv()
            top, total = merge(target[...])
            result = out_ref if index == 1 else middle
            result[...] = jnp.zeros(result.shape, result.dtype)
            result[0:1, :] = top
            result[1:2, :] = total

    count = max(counts.values())
    return pl.pallas_call(
        kernel,
        out_shape=jax.ShapeDtypeStruct(tile.shape, tile.dtype),
        in_specs=[pl.BlockSpec(memory_space=pltpu.VMEM)],
        out_specs=pl.BlockSpec(memory_space=pltpu.VMEM),
        scratch_shapes=[
            pltpu.VMEM((counts["mp"],) + tile.shape, tile.dtype),
            pltpu.VMEM((counts["dp"],) + tile.shape, tile.dtype),
            pltpu.VMEM(tile.shape, tile.dtype),
            pltpu.SemaphoreType.DMA((2, count)),
            pltpu.SemaphoreType.DMA((2, count)),
        ],
        compiler_params=pltpu.CompilerParams(collective_id=tag, has_side_effects=True),
    )(tile)


def tail_exchange(blocks, end_parts, skip_ends, gain, counts, tag):
    rows = end_parts.shape[0]

    def kernel(blocks_ref, parts_ref, skip_ref, gain_ref, swapped_ref, head_ref,
               parts_held, normed, send_sem, recv_sem):
        barrier = pltpu.get_barrier_semaphore()
        for axis in ("mp", "dp"):
            me = lax.axis_index(axis)
            for step in range(1, counts[axis]):
                peer = lax.rem(me + step, counts[axis])
                pl.semaphore_signal(barrier, 1, device_id={axis: peer},
                                    device_id_type=pl.DeviceIdType.MESH)
        pl.semaphore_wait(barrier, counts["mp"] + counts["dp"] - 2)
        me = lax.axis_index("mp")
        block_copies, part_copies = [], []
        for step in range(1, counts["mp"]):
            peer = lax.rem(me + step, counts["mp"])
            copy = pltpu.make_async_remote_copy(
                src_ref=parts_ref, dst_ref=parts_held.at[me],
                send_sem=send_sem.at[0, step], recv_sem=recv_sem.at[0, step],
                device_id={"mp": peer}, device_id_type=pl.DeviceIdType.MESH)
            copy.start()
            part_copies.append(copy)
        parts_held[me] = parts_ref[...]
        for copy in part_copies:
            copy.wait_send()
            copy.wait_recv()
        total = jnp.sum(parts_held[...].astype(jnp.float32), axis=0)
        end_rows = skip_ref[...] + branch_scale * total
        squares = jnp.sum(end_rows * end_rows, axis=1, keepdims=True)
        normed[...] = (
            end_rows * lax.rsqrt(squares / EMBED_DIMENSION + epsilon) * gain_ref[...]
        ).astype(normed.dtype)
        group = lax.axis_index("dp")
        head_copies = []
        for step in range(1, counts["dp"]):
            peer = lax.rem(group + step, counts["dp"])
            copy = pltpu.make_async_remote_copy(
                src_ref=normed, dst_ref=head_ref.at[group],
                send_sem=send_sem.at[2, step], recv_sem=recv_sem.at[2, step],
                device_id={"dp": peer}, device_id_type=pl.DeviceIdType.MESH)
            copy.start()
            head_copies.append(copy)
        for step in range(1, counts["mp"]):
            peer = lax.rem(me + step, counts["mp"])
            copy = pltpu.make_async_remote_copy(
                src_ref=blocks_ref.at[peer], dst_ref=swapped_ref.at[me],
                send_sem=send_sem.at[1, step], recv_sem=recv_sem.at[1, step],
                device_id={"mp": peer}, device_id_type=pl.DeviceIdType.MESH)
            copy.start()
            block_copies.append(copy)
        head_ref[group] = normed[...]
        swapped_ref[me] = blocks_ref[me]
        for copy in block_copies + head_copies:
            copy.wait_send()
            copy.wait_recv()

    count = max(counts.values())
    return pl.pallas_call(
        kernel,
        out_shape=[
            jax.ShapeDtypeStruct(blocks.shape, blocks.dtype),
            jax.ShapeDtypeStruct((counts["dp"], rows, EMBED_DIMENSION), jnp.bfloat16),
        ],
        in_specs=[pl.BlockSpec(memory_space=pltpu.VMEM)] * 4,
        out_specs=[pl.BlockSpec(memory_space=pltpu.VMEM)] * 2,
        scratch_shapes=[
            pltpu.VMEM((counts["mp"],) + end_parts.shape, end_parts.dtype),
            pltpu.VMEM((rows, EMBED_DIMENSION), jnp.bfloat16),
            pltpu.SemaphoreType.DMA((3, count)),
            pltpu.SemaphoreType.DMA((3, count)),
        ],
        compiler_params=pltpu.CompilerParams(collective_id=tag, has_side_effects=True),
    )(blocks, end_parts, skip_ends, gain)


def body(
    skip_stream_arriving,
    chosen_specialists,
    sequence_piece_tallies,
    premix_rmsnorm_gain,
    dispatcher_weights,
    specialist_switch_weights,
    specialist_expand_weights,
    specialist_contract_weights,
    terminal_rmsnorm_gain,
    lexicon_projector_weights,
    softness_per_sequence,
):
    tok_rows = skip_stream_arriving.shape[0]
    experts = specialist_switch_weights.shape[0]
    columns_count = lax.axis_size("mp")
    groups = lax.axis_size("dp")
    local_squares = jnp.sum(skip_stream_arriving * skip_stream_arriving, axis=1)
    squares = jnp.sum(axis_gather(local_squares[None], "mp", columns_count, 0), axis=(0, 1))
    normed_local = (
        skip_stream_arriving
        * lax.rsqrt(squares / EMBED_DIMENSION + epsilon)[:, None]
        * premix_rmsnorm_gain
    ).astype(jnp.bfloat16)
    features_t = axis_gather(normed_local.T, "mp", columns_count, 5).reshape(
        EMBED_DIMENSION, tok_rows
    )
    by_rows = (((0,), (0,)), ((), ()))
    router = lax.dot_general(
        features_t, dispatcher_weights, by_rows, preferred_element_type=jnp.float32
    )
    mixing = jax.nn.softmax(jnp.take_along_axis(router, chosen_specialists, axis=1), axis=1)
    all_weights = lax.all_gather(
        jnp.stack(
            [
                specialist_switch_weights,
                specialist_expand_weights,
                jnp.swapaxes(specialist_contract_weights, 1, 2),
            ],
            axis=1,
        ),
        "dp", axis=2, tiled=True,
    )
    combined_t = jnp.zeros((EMBED_DIMENSION, tok_rows), jnp.float32)
    for expert in range(experts):
        weight = jnp.where(chosen_specialists[:, 0] == expert, mixing[:, 0], 0.0) + jnp.where(
            chosen_specialists[:, 1] == expert, mixing[:, 1], 0.0
        )
        gate_t = lax.dot_general(
            all_weights[expert, 0], features_t, by_rows, preferred_element_type=jnp.float32
        )
        up_t = lax.dot_general(
            all_weights[expert, 1], features_t, by_rows, preferred_element_type=jnp.float32
        )
        act_t = (jax.nn.silu(gate_t) * up_t).astype(jnp.bfloat16)
        down_t = jnp.dot(all_weights[expert, 2], act_t, preferred_element_type=jnp.float32)
        combined_t = combined_t + down_t * weight[None, :]
    ends_index = jnp.cumsum(sequence_piece_tallies[0], dtype=jnp.int32) - 1
    partial_t = combined_t.astype(jnp.bfloat16)
    column_blocks = partial_t.reshape(columns_count, -1, tok_rows)
    skip_ends = (
        axis_gather(skip_stream_arriving[ends_index], "mp", columns_count, 6)
        .transpose(1, 0, 2)
        .reshape(ends_index.shape[0], EMBED_DIMENSION)
    )
    swapped, head_rows = tail_exchange(
        column_blocks,
        partial_t[:, ends_index].T,
        skip_ends,
        terminal_rmsnorm_gain[None],
        {"mp": columns_count, "dp": groups},
        7,
    )
    branch = jnp.sum(swapped.astype(jnp.float32), axis=0).T
    new_hidden = skip_stream_arriving + branch_scale * branch
    lexicon_projector_feed = head_rows.reshape(groups * ends_index.shape[0], EMBED_DIMENSION)
    lexicon_logit_values = jnp.dot(
        lexicon_projector_feed, lexicon_projector_weights, preferred_element_type=jnp.float32
    ) / (EMBED_DIMENSION / 256.0 * softness_per_sequence[:, None])
    local_max = jnp.max(lexicon_logit_values, axis=1)
    local_sum = jnp.sum(jnp.exp(lexicon_logit_values - local_max[:, None]), axis=1)
    requests = local_max.shape[0]
    tile = jnp.zeros((8, 128), jnp.float32)
    tile = tile.at[0, :requests].set(local_max).at[1, :requests].set(local_sum)
    merged = stats_combine(tile, {"mp": columns_count, "dp": groups}, 3)
    largest, total_exp = merged[0, :requests], merged[1, :requests]
    logprobs = lexicon_logit_values - largest[:, None] - jnp.log(total_exp)[:, None]
    return (new_hidden, logprobs)


def solution(mesh):
    return jax.shard_map(
        body,
        mesh=mesh,
        in_specs=(
            P("dp", "mp"),
            P("dp", None),
            P("dp", None),
            P("mp"),
            P(),
            P(None, "dp", "mp"),
            P(None, "dp", "mp"),
            P(None, "mp", "dp"),
            P(),
            P(None, ("dp", "mp")),
            P(),
        ),
        out_specs=(P("dp", "mp"), P(None, ("dp", "mp"))),
        check_vma=False,
    )
```

```python
import math

import jax
import jax.numpy as jnp
from jax import lax
from jax.experimental import pallas as pl
from jax.experimental.pallas import tpu as pltpu
from jax.sharding import PartitionSpec as P

EMBED_DIMENSION = 2304


branch_scale = 1.4 / math.sqrt(40.0)
epsilon = 1e-05


def axis_share(parts, axis, count, tag):
    arrays = [array for array, _ in parts]
    splits = [split for _, split in parts]
    width = len(arrays)

    def kernel(*refs):
        sources, targets = refs[:width], refs[width:2 * width]
        send_sem, recv_sem = refs[2 * width:]
        me = lax.axis_index(axis)
        barrier = pltpu.get_barrier_semaphore()
        for step in range(1, count):
            peer = lax.rem(me + step, count)
            pl.semaphore_signal(barrier, 1, device_id={axis: peer},
                                device_id_type=pl.DeviceIdType.MESH)
        pl.semaphore_wait(barrier, count - 1)
        copies = []
        for step in range(1, count):
            peer = lax.rem(me + step, count)
            for index in range(width):
                source = sources[index].at[peer] if splits[index] else sources[index]
                copy = pltpu.make_async_remote_copy(
                    src_ref=source, dst_ref=targets[index].at[me],
                    send_sem=send_sem.at[index, step], recv_sem=recv_sem.at[index, step],
                    device_id={axis: peer}, device_id_type=pl.DeviceIdType.MESH)
                copy.start()
                copies.append(copy)
        for index in range(width):
            if splits[index]:
                targets[index][me] = sources[index][me]
            else:
                targets[index][me] = sources[index][...]
        for copy in copies:
            copy.wait_send()
            copy.wait_recv()

    return pl.pallas_call(
        kernel,
        out_shape=[
            jax.ShapeDtypeStruct(array.shape if split else (count,) + array.shape, array.dtype)
            for array, split in parts
        ],
        in_specs=[pl.BlockSpec(memory_space=pltpu.VMEM)] * width,
        out_specs=[pl.BlockSpec(memory_space=pltpu.VMEM)] * width,
        scratch_shapes=[
            pltpu.SemaphoreType.DMA((width, count)),
            pltpu.SemaphoreType.DMA((width, count)),
        ],
        compiler_params=pltpu.CompilerParams(collective_id=tag, has_side_effects=True),
    )(*arrays)


def axis_gather(block, axis, count, tag):
    return axis_share([(block, False)], axis, count, tag)[0]


def stats_combine(tile, counts, tag):
    axes = ("mp", "dp")

    def merge(buffer):
        top = jnp.max(buffer[:, 0, :], axis=0, keepdims=True)
        total = jnp.sum(buffer[:, 1, :] * jnp.exp(buffer[:, 0, :] - top), axis=0, keepdims=True)
        return top, total

    def kernel(x_ref, out_ref, first, second, middle, send_sem, recv_sem):
        barrier = pltpu.get_barrier_semaphore()
        for axis in axes:
            me = lax.axis_index(axis)
            for step in range(1, counts[axis]):
                peer = lax.rem(me + step, counts[axis])
                pl.semaphore_signal(barrier, 1, device_id={axis: peer},
                                    device_id_type=pl.DeviceIdType.MESH)
        pl.semaphore_wait(barrier, sum(counts[axis] - 1 for axis in axes))
        stages = ((x_ref, first), (middle, second))
        for index, axis in enumerate(axes):
            source, target = stages[index]
            me = lax.axis_index(axis)
            copies = []
            for step in range(1, counts[axis]):
                peer = lax.rem(me + step, counts[axis])
                copy = pltpu.make_async_remote_copy(
                    src_ref=source, dst_ref=target.at[me],
                    send_sem=send_sem.at[index, step], recv_sem=recv_sem.at[index, step],
                    device_id={axis: peer}, device_id_type=pl.DeviceIdType.MESH)
                copy.start()
                copies.append(copy)
            target[me] = source[...]
            for copy in copies:
                copy.wait_send()
                copy.wait_recv()
            top, total = merge(target[...])
            result = out_ref if index == 1 else middle
            result[...] = jnp.zeros(result.shape, result.dtype)
            result[0:1, :] = top
            result[1:2, :] = total

    count = max(counts.values())
    return pl.pallas_call(
        kernel,
        out_shape=jax.ShapeDtypeStruct(tile.shape, tile.dtype),
        in_specs=[pl.BlockSpec(memory_space=pltpu.VMEM)],
        out_specs=pl.BlockSpec(memory_space=pltpu.VMEM),
        scratch_shapes=[
            pltpu.VMEM((counts["mp"],) + tile.shape, tile.dtype),
            pltpu.VMEM((counts["dp"],) + tile.shape, tile.dtype),
            pltpu.VMEM(tile.shape, tile.dtype),
            pltpu.SemaphoreType.DMA((2, count)),
            pltpu.SemaphoreType.DMA((2, count)),
        ],
        compiler_params=pltpu.CompilerParams(collective_id=tag, has_side_effects=True),
    )(tile)


def tail_exchange(blocks, end_parts, skip_ends, gain, counts, tag):
    rows = end_parts.shape[0]

    def kernel(blocks_ref, parts_ref, skip_ref, gain_ref, swapped_ref, head_ref,
               parts_held, normed, send_sem, recv_sem):
        barrier = pltpu.get_barrier_semaphore()
        for axis in ("mp", "dp"):
            me = lax.axis_index(axis)
            for step in range(1, counts[axis]):
                peer = lax.rem(me + step, counts[axis])
                pl.semaphore_signal(barrier, 1, device_id={axis: peer},
                                    device_id_type=pl.DeviceIdType.MESH)
        pl.semaphore_wait(barrier, counts["mp"] + counts["dp"] - 2)
        me = lax.axis_index("mp")
        block_copies, part_copies = [], []
        for step in range(1, counts["mp"]):
            peer = lax.rem(me + step, counts["mp"])
            copy = pltpu.make_async_remote_copy(
                src_ref=parts_ref, dst_ref=parts_held.at[me],
                send_sem=send_sem.at[0, step], recv_sem=recv_sem.at[0, step],
                device_id={"mp": peer}, device_id_type=pl.DeviceIdType.MESH)
            copy.start()
            part_copies.append(copy)
        for step in range(1, counts["mp"]):
            peer = lax.rem(me + step, counts["mp"])
            copy = pltpu.make_async_remote_copy(
                src_ref=blocks_ref.at[peer], dst_ref=swapped_ref.at[me],
                send_sem=send_sem.at[1, step], recv_sem=recv_sem.at[1, step],
                device_id={"mp": peer}, device_id_type=pl.DeviceIdType.MESH)
            copy.start()
            block_copies.append(copy)
        parts_held[me] = parts_ref[...]
        swapped_ref[me] = blocks_ref[me]
        for copy in part_copies:
            copy.wait_send()
            copy.wait_recv()
        total = jnp.sum(parts_held[...].astype(jnp.float32), axis=0)
        end_rows = skip_ref[...] + branch_scale * total
        squares = jnp.sum(end_rows * end_rows, axis=1, keepdims=True)
        normed[...] = (
            end_rows * lax.rsqrt(squares / EMBED_DIMENSION + epsilon) * gain_ref[...]
        ).astype(normed.dtype)
        group = lax.axis_index("dp")
        head_copies = []
        for step in range(1, counts["dp"]):
            peer = lax.rem(group + step, counts["dp"])
            copy = pltpu.make_async_remote_copy(
                src_ref=normed, dst_ref=head_ref.at[group],
                send_sem=send_sem.at[2, step], recv_sem=recv_sem.at[2, step],
                device_id={"dp": peer}, device_id_type=pl.DeviceIdType.MESH)
            copy.start()
            head_copies.append(copy)
        head_ref[group] = normed[...]
        for copy in block_copies + head_copies:
            copy.wait_send()
            copy.wait_recv()

    count = max(counts.values())
    return pl.pallas_call(
        kernel,
        out_shape=[
            jax.ShapeDtypeStruct(blocks.shape, blocks.dtype),
            jax.ShapeDtypeStruct((counts["dp"], rows, EMBED_DIMENSION), jnp.bfloat16),
        ],
        in_specs=[pl.BlockSpec(memory_space=pltpu.VMEM)] * 4,
        out_specs=[pl.BlockSpec(memory_space=pltpu.VMEM)] * 2,
        scratch_shapes=[
            pltpu.VMEM((counts["mp"],) + end_parts.shape, end_parts.dtype),
            pltpu.VMEM((rows, EMBED_DIMENSION), jnp.bfloat16),
            pltpu.SemaphoreType.DMA((3, count)),
            pltpu.SemaphoreType.DMA((3, count)),
        ],
        compiler_params=pltpu.CompilerParams(collective_id=tag, has_side_effects=True),
    )(blocks, end_parts, skip_ends, gain)


def body(
    skip_stream_arriving,
    chosen_specialists,
    sequence_piece_tallies,
    premix_rmsnorm_gain,
    dispatcher_weights,
    specialist_switch_weights,
    specialist_expand_weights,
    specialist_contract_weights,
    terminal_rmsnorm_gain,
    lexicon_projector_weights,
    softness_per_sequence,
):
    tok_rows = skip_stream_arriving.shape[0]
    experts = specialist_switch_weights.shape[0]
    columns_count = lax.axis_size("mp")
    groups = lax.axis_size("dp")
    local_squares = jnp.sum(skip_stream_arriving * skip_stream_arriving, axis=1)
    ends_index = jnp.cumsum(sequence_piece_tallies[0], dtype=jnp.int32) - 1
    held_squares, skip_ends = axis_share(
        [(local_squares[None], False), (skip_stream_arriving[ends_index], False)],
        "mp", columns_count, 0,
    )
    squares = jnp.sum(held_squares, axis=(0, 1))
    skip_ends = skip_ends.transpose(1, 0, 2).reshape(ends_index.shape[0], EMBED_DIMENSION)
    normed_local = (
        skip_stream_arriving
        * lax.rsqrt(squares / EMBED_DIMENSION + epsilon)[:, None]
        * premix_rmsnorm_gain
    ).astype(jnp.bfloat16)
    features_t = axis_gather(normed_local.T, "mp", columns_count, 5).reshape(
        EMBED_DIMENSION, tok_rows
    )
    by_rows = (((0,), (0,)), ((), ()))
    router = lax.dot_general(
        features_t, dispatcher_weights, by_rows, preferred_element_type=jnp.float32
    )
    mixing = jax.nn.softmax(jnp.take_along_axis(router, chosen_specialists, axis=1), axis=1)
    all_weights = lax.all_gather(
        jnp.stack(
            [
                specialist_switch_weights,
                specialist_expand_weights,
                jnp.swapaxes(specialist_contract_weights, 1, 2),
            ],
            axis=1,
        ),
        "dp", axis=2, tiled=True,
    )
    combined_t = jnp.zeros((EMBED_DIMENSION, tok_rows), jnp.float32)
    for expert in range(experts):
        weight = jnp.where(chosen_specialists[:, 0] == expert, mixing[:, 0], 0.0) + jnp.where(
            chosen_specialists[:, 1] == expert, mixing[:, 1], 0.0
        )
        gate_t = lax.dot_general(
            all_weights[expert, 0], features_t, by_rows, preferred_element_type=jnp.float32
        )
        up_t = lax.dot_general(
            all_weights[expert, 1], features_t, by_rows, preferred_element_type=jnp.float32
        )
        act_t = (jax.nn.silu(gate_t) * up_t).astype(jnp.bfloat16)
        down_t = jnp.dot(all_weights[expert, 2], act_t, preferred_element_type=jnp.float32)
        combined_t = combined_t + down_t * weight[None, :]
    partial_t = combined_t.astype(jnp.bfloat16)
    column_blocks = partial_t.reshape(columns_count, -1, tok_rows)
    swapped, head_rows = tail_exchange(
        column_blocks,
        partial_t[:, ends_index].T,
        skip_ends,
        terminal_rmsnorm_gain[None],
        {"mp": columns_count, "dp": groups},
        7,
    )
    branch = jnp.sum(swapped.astype(jnp.float32), axis=0).T
    new_hidden = skip_stream_arriving + branch_scale * branch
    lexicon_projector_feed = head_rows.reshape(groups * ends_index.shape[0], EMBED_DIMENSION)
    lexicon_logit_values = jnp.dot(
        lexicon_projector_feed, lexicon_projector_weights, preferred_element_type=jnp.float32
    ) / (EMBED_DIMENSION / 256.0 * softness_per_sequence[:, None])
    local_max = jnp.max(lexicon_logit_values, axis=1)
    local_sum = jnp.sum(jnp.exp(lexicon_logit_values - local_max[:, None]), axis=1)
    requests = local_max.shape[0]
    tile = jnp.zeros((8, 128), jnp.float32)
    tile = tile.at[0, :requests].set(local_max).at[1, :requests].set(local_sum)
    merged = stats_combine(tile, {"mp": columns_count, "dp": groups}, 3)
    largest, total_exp = merged[0, :requests], merged[1, :requests]
    logprobs = lexicon_logit_values - largest[:, None] - jnp.log(total_exp)[:, None]
    return (new_hidden, logprobs)


def solution(mesh):
    return jax.shard_map(
        body,
        mesh=mesh,
        in_specs=(
            P("dp", "mp"),
            P("dp", None),
            P("dp", None),
            P("mp"),
            P(),
            P(None, "dp", "mp"),
            P(None, "dp", "mp"),
            P(None, "mp", "dp"),
            P(),
            P(None, ("dp", "mp")),
            P(),
        ),
        out_specs=(P("dp", "mp"), P(None, ("dp", "mp"))),
        check_vma=False,
    )
```

```python
import math

import jax
import jax.numpy as jnp
from jax import lax
from jax.experimental import pallas as pl
from jax.experimental.pallas import tpu as pltpu
from jax.sharding import PartitionSpec as P

EMBED_DIMENSION = 2304


branch_scale = 1.4 / math.sqrt(40.0)
epsilon = 1e-05


def axis_share(parts, axis, count, tag):
    arrays = [array for array, _ in parts]
    splits = [split for _, split in parts]
    width = len(arrays)

    def kernel(*refs):
        sources, targets = refs[:width], refs[width:2 * width]
        send_sem, recv_sem = refs[2 * width:]
        me = lax.axis_index(axis)
        barrier = pltpu.get_barrier_semaphore()
        for step in range(1, count):
            peer = lax.rem(me + step, count)
            pl.semaphore_signal(barrier, 1, device_id={axis: peer},
                                device_id_type=pl.DeviceIdType.MESH)
        pl.semaphore_wait(barrier, count - 1)
        copies = []
        for step in range(1, count):
            peer = lax.rem(me + step, count)
            for index in range(width):
                source = sources[index].at[peer] if splits[index] else sources[index]
                copy = pltpu.make_async_remote_copy(
                    src_ref=source, dst_ref=targets[index].at[me],
                    send_sem=send_sem.at[index, step], recv_sem=recv_sem.at[index, step],
                    device_id={axis: peer}, device_id_type=pl.DeviceIdType.MESH)
                copy.start()
                copies.append(copy)
        for index in range(width):
            if splits[index]:
                targets[index][me] = sources[index][me]
            else:
                targets[index][me] = sources[index][...]
        for copy in copies:
            copy.wait_send()
            copy.wait_recv()

    return pl.pallas_call(
        kernel,
        out_shape=[
            jax.ShapeDtypeStruct(array.shape if split else (count,) + array.shape, array.dtype)
            for array, split in parts
        ],
        in_specs=[pl.BlockSpec(memory_space=pltpu.VMEM)] * width,
        out_specs=[pl.BlockSpec(memory_space=pltpu.VMEM)] * width,
        scratch_shapes=[
            pltpu.SemaphoreType.DMA((width, count)),
            pltpu.SemaphoreType.DMA((width, count)),
        ],
        compiler_params=pltpu.CompilerParams(collective_id=tag, has_side_effects=True),
    )(*arrays)


def axis_gather(block, axis, count, tag):
    return axis_share([(block, False)], axis, count, tag)[0]


def stats_combine(tile, counts, tag):
    axes = ("mp", "dp")

    def merge(buffer):
        top = jnp.max(buffer[:, 0, :], axis=0, keepdims=True)
        total = jnp.sum(buffer[:, 1, :] * jnp.exp(buffer[:, 0, :] - top), axis=0, keepdims=True)
        return top, total

    def kernel(x_ref, out_ref, first, second, middle, send_sem, recv_sem):
        barrier = pltpu.get_barrier_semaphore()
        for axis in axes:
            me = lax.axis_index(axis)
            for step in range(1, counts[axis]):
                peer = lax.rem(me + step, counts[axis])
                pl.semaphore_signal(barrier, 1, device_id={axis: peer},
                                    device_id_type=pl.DeviceIdType.MESH)
        pl.semaphore_wait(barrier, sum(counts[axis] - 1 for axis in axes))
        stages = ((x_ref, first), (middle, second))
        for index, axis in enumerate(axes):
            source, target = stages[index]
            me = lax.axis_index(axis)
            copies = []
            for step in range(1, counts[axis]):
                peer = lax.rem(me + step, counts[axis])
                copy = pltpu.make_async_remote_copy(
                    src_ref=source, dst_ref=target.at[me],
                    send_sem=send_sem.at[index, step], recv_sem=recv_sem.at[index, step],
                    device_id={axis: peer}, device_id_type=pl.DeviceIdType.MESH)
                copy.start()
                copies.append(copy)
            target[me] = source[...]
            for copy in copies:
                copy.wait_send()
                copy.wait_recv()
            top, total = merge(target[...])
            result = out_ref if index == 1 else middle
            result[...] = jnp.zeros(result.shape, result.dtype)
            result[0:1, :] = top
            result[1:2, :] = total

    count = max(counts.values())
    return pl.pallas_call(
        kernel,
        out_shape=jax.ShapeDtypeStruct(tile.shape, tile.dtype),
        in_specs=[pl.BlockSpec(memory_space=pltpu.VMEM)],
        out_specs=pl.BlockSpec(memory_space=pltpu.VMEM),
        scratch_shapes=[
            pltpu.VMEM((counts["mp"],) + tile.shape, tile.dtype),
            pltpu.VMEM((counts["dp"],) + tile.shape, tile.dtype),
            pltpu.VMEM(tile.shape, tile.dtype),
            pltpu.SemaphoreType.DMA((2, count)),
            pltpu.SemaphoreType.DMA((2, count)),
        ],
        compiler_params=pltpu.CompilerParams(collective_id=tag, has_side_effects=True),
    )(tile)


def tail_exchange(blocks, end_parts, skip_ends, gain, counts, tag):
    rows = end_parts.shape[0]

    def kernel(blocks_ref, parts_ref, skip_ref, gain_ref, swapped_ref, head_ref,
               parts_held, normed, send_sem, recv_sem):
        barrier = pltpu.get_barrier_semaphore()
        for axis in ("mp", "dp"):
            me = lax.axis_index(axis)
            for step in range(1, counts[axis]):
                peer = lax.rem(me + step, counts[axis])
                pl.semaphore_signal(barrier, 1, device_id={axis: peer},
                                    device_id_type=pl.DeviceIdType.MESH)
        pl.semaphore_wait(barrier, counts["mp"] + counts["dp"] - 2)
        me = lax.axis_index("mp")
        block_copies, part_copies = [], []
        for step in range(1, counts["mp"]):
            peer = lax.rem(me + step, counts["mp"])
            copy = pltpu.make_async_remote_copy(
                src_ref=parts_ref, dst_ref=parts_held.at[me],
                send_sem=send_sem.at[0, step], recv_sem=recv_sem.at[0, step],
                device_id={"mp": peer}, device_id_type=pl.DeviceIdType.MESH)
            copy.start()
            part_copies.append(copy)
        width = blocks.shape[2] // 2

        def send_blocks(half, slot):
            for step in range(1, counts["mp"]):
                peer = lax.rem(me + step, counts["mp"])
                lanes = pl.ds(half * width, width)
                copy = pltpu.make_async_remote_copy(
                    src_ref=blocks_ref.at[peer, :, lanes], dst_ref=swapped_ref.at[me, :, lanes],
                    send_sem=send_sem.at[slot, step], recv_sem=recv_sem.at[slot, step],
                    device_id={"mp": peer}, device_id_type=pl.DeviceIdType.MESH)
                copy.start()
                block_copies.append(copy)

        send_blocks(0, 1)
        parts_held[me] = parts_ref[...]
        swapped_ref[me] = blocks_ref[me]
        for copy in part_copies:
            copy.wait_send()
            copy.wait_recv()
        total = jnp.sum(parts_held[...].astype(jnp.float32), axis=0)
        end_rows = skip_ref[...] + branch_scale * total
        squares = jnp.sum(end_rows * end_rows, axis=1, keepdims=True)
        normed[...] = (
            end_rows * lax.rsqrt(squares / EMBED_DIMENSION + epsilon) * gain_ref[...]
        ).astype(normed.dtype)
        group = lax.axis_index("dp")
        head_copies = []
        for step in range(1, counts["dp"]):
            peer = lax.rem(group + step, counts["dp"])
            copy = pltpu.make_async_remote_copy(
                src_ref=normed, dst_ref=head_ref.at[group],
                send_sem=send_sem.at[2, step], recv_sem=recv_sem.at[2, step],
                device_id={"dp": peer}, device_id_type=pl.DeviceIdType.MESH)
            copy.start()
            head_copies.append(copy)
        send_blocks(1, 3)
        head_ref[group] = normed[...]
        for copy in block_copies + head_copies:
            copy.wait_send()
            copy.wait_recv()

    count = max(counts.values())
    return pl.pallas_call(
        kernel,
        out_shape=[
            jax.ShapeDtypeStruct(blocks.shape, blocks.dtype),
            jax.ShapeDtypeStruct((counts["dp"], rows, EMBED_DIMENSION), jnp.bfloat16),
        ],
        in_specs=[pl.BlockSpec(memory_space=pltpu.VMEM)] * 4,
        out_specs=[pl.BlockSpec(memory_space=pltpu.VMEM)] * 2,
        scratch_shapes=[
            pltpu.VMEM((counts["mp"],) + end_parts.shape, end_parts.dtype),
            pltpu.VMEM((rows, EMBED_DIMENSION), jnp.bfloat16),
            pltpu.SemaphoreType.DMA((4, count)),
            pltpu.SemaphoreType.DMA((4, count)),
        ],
        compiler_params=pltpu.CompilerParams(collective_id=tag, has_side_effects=True),
    )(blocks, end_parts, skip_ends, gain)


def body(
    skip_stream_arriving,
    chosen_specialists,
    sequence_piece_tallies,
    premix_rmsnorm_gain,
    dispatcher_weights,
    specialist_switch_weights,
    specialist_expand_weights,
    specialist_contract_weights,
    terminal_rmsnorm_gain,
    lexicon_projector_weights,
    softness_per_sequence,
):
    tok_rows = skip_stream_arriving.shape[0]
    experts = specialist_switch_weights.shape[0]
    columns_count = lax.axis_size("mp")
    groups = lax.axis_size("dp")
    local_squares = jnp.sum(skip_stream_arriving * skip_stream_arriving, axis=1)
    ends_index = jnp.cumsum(sequence_piece_tallies[0], dtype=jnp.int32) - 1
    held_squares, skip_ends = axis_share(
        [(local_squares[None], False), (skip_stream_arriving[ends_index], False)],
        "mp", columns_count, 0,
    )
    squares = jnp.sum(held_squares, axis=(0, 1))
    skip_ends = skip_ends.transpose(1, 0, 2).reshape(ends_index.shape[0], EMBED_DIMENSION)
    normed_local = (
        skip_stream_arriving
        * lax.rsqrt(squares / EMBED_DIMENSION + epsilon)[:, None]
        * premix_rmsnorm_gain
    ).astype(jnp.bfloat16)
    features_t = axis_gather(normed_local.T, "mp", columns_count, 5).reshape(
        EMBED_DIMENSION, tok_rows
    )
    by_rows = (((0,), (0,)), ((), ()))
    router = lax.dot_general(
        features_t, dispatcher_weights, by_rows, preferred_element_type=jnp.float32
    )
    mixing = jax.nn.softmax(jnp.take_along_axis(router, chosen_specialists, axis=1), axis=1)
    all_weights = lax.all_gather(
        jnp.stack(
            [
                specialist_switch_weights,
                specialist_expand_weights,
                jnp.swapaxes(specialist_contract_weights, 1, 2),
            ],
            axis=1,
        ),
        "dp", axis=2, tiled=True,
    )
    combined_t = jnp.zeros((EMBED_DIMENSION, tok_rows), jnp.float32)
    for expert in range(experts):
        weight = jnp.where(chosen_specialists[:, 0] == expert, mixing[:, 0], 0.0) + jnp.where(
            chosen_specialists[:, 1] == expert, mixing[:, 1], 0.0
        )
        gate_t = lax.dot_general(
            all_weights[expert, 0], features_t, by_rows, preferred_element_type=jnp.float32
        )
        up_t = lax.dot_general(
            all_weights[expert, 1], features_t, by_rows, preferred_element_type=jnp.float32
        )
        act_t = (jax.nn.silu(gate_t) * up_t).astype(jnp.bfloat16)
        down_t = jnp.dot(all_weights[expert, 2], act_t, preferred_element_type=jnp.float32)
        combined_t = combined_t + down_t * weight[None, :]
    partial_t = combined_t.astype(jnp.bfloat16)
    column_blocks = partial_t.reshape(columns_count, -1, tok_rows)
    swapped, head_rows = tail_exchange(
        column_blocks,
        partial_t[:, ends_index].T,
        skip_ends,
        terminal_rmsnorm_gain[None],
        {"mp": columns_count, "dp": groups},
        7,
    )
    branch = jnp.sum(swapped.astype(jnp.float32), axis=0).T
    new_hidden = skip_stream_arriving + branch_scale * branch
    lexicon_projector_feed = head_rows.reshape(groups * ends_index.shape[0], EMBED_DIMENSION)
    lexicon_logit_values = jnp.dot(
        lexicon_projector_feed, lexicon_projector_weights, preferred_element_type=jnp.float32
    ) / (EMBED_DIMENSION / 256.0 * softness_per_sequence[:, None])
    local_max = jnp.max(lexicon_logit_values, axis=1)
    local_sum = jnp.sum(jnp.exp(lexicon_logit_values - local_max[:, None]), axis=1)
    requests = local_max.shape[0]
    tile = jnp.zeros((8, 128), jnp.float32)
    tile = tile.at[0, :requests].set(local_max).at[1, :requests].set(local_sum)
    merged = stats_combine(tile, {"mp": columns_count, "dp": groups}, 3)
    largest, total_exp = merged[0, :requests], merged[1, :requests]
    logprobs = lexicon_logit_values - largest[:, None] - jnp.log(total_exp)[:, None]
    return (new_hidden, logprobs)


def solution(mesh):
    return jax.shard_map(
        body,
        mesh=mesh,
        in_specs=(
            P("dp", "mp"),
            P("dp", None),
            P("dp", None),
            P("mp"),
            P(),
            P(None, "dp", "mp"),
            P(None, "dp", "mp"),
            P(None, "mp", "dp"),
            P(),
            P(None, ("dp", "mp")),
            P(),
        ),
        out_specs=(P("dp", "mp"), P(None, ("dp", "mp"))),
        check_vma=False,
    )
```
